32 devices in a mesh: band: 8 (over z, x), rep: 4 (over y, core).
Axes of the slice: x: 2, y: 2, z: 4, core: 2. Of those that a mesh axis runs over, the one named last changes fastest.
Arguments:
- feats: bfloat16 [131072, 128], P(('band', 'rep')), may hold values from -6 to 6
- tile_vals: bfloat16 [1024, 3, 128, 128], P(('band', 'rep')), may hold values from -0.3125 to 0.3125
- tile_offs: int32 [1024, 3], P(('band', 'rep')), may hold values from -16 to 16, as said below
- w_in: bfloat16 [2, 256, 128], replicated, may hold values from -0.375 to 0.375
- bias_in: float32 [2, 128], replicated, may hold values from -3 to 3
- w_out: bfloat16 [2, 128, 128], replicated, may hold values from -0.5 to 0.5
- gain: float32 [2, 128], replicated, may hold values from 0.1 to 1.9
- cot: bfloat16 [131072, 128], P(('band', 'rep')), may hold values from -6 to 6
Outputs:
- out_feats: bfloat16 [131072, 128], P(('band', 'rep'))
- grad_feats: float32 [131072, 128], P(('band', 'rep'))
- grad_w_in: float32 [2, 256, 128], replicated
- grad_bias_in: float32 [2, 128], replicated
- grad_w_out: float32 [2, 128, 128], replicated
- grad_gain: float32 [2, 128], replicated
The draws below stay inside these ranges and needn't reach their ends.
Inputs may be any that keep to these rules, and one draw needn't show every extreme that they name: `tile_offs`: in every block row slot 0 is 0, slot 1 lies in -16 to -1 and slot 2 in 1 to 16; block rows whose index is a multiple of 16 have -16 and 16.
All inputs are finite; a program needn't handle non-finite values.
Results may differ from the reference program's by a relative error of at most 0.0085.
Values may be sent and summed in bfloat16 or wider, within the bound.
No kernel may reach another device: no remote copies, remote signals or barrier semaphores. Data moves between devices by JAX's collectives and lax.ppermute only.
A program may use at most 128 MiB of HBM per device.

```python
import math
import jax
import jax.numpy as jnp
from jax import lax

D = 128
HID = 128
BLK = 128
TPR = 3
HALO_BLK = 16
LAYERS = 2
NODES = 131072
BLOCKS = 1024
N_BAND = 8
N_REP = 4


def draw_tile_offs(key, part):
    key_low, key_high = jax.random.split(key)
    lower_off = -jax.random.randint(key_low, (BLOCKS,), 1, HALO_BLK + 1, dtype=jnp.int32)
    upper_off = jax.random.randint(key_high, (BLOCKS,), 1, HALO_BLK + 1, dtype=jnp.int32)
    marked = jnp.arange(BLOCKS, dtype=jnp.int32) % HALO_BLK == 0
    lower_off = jnp.where(marked, -HALO_BLK, lower_off)
    upper_off = jnp.where(marked, HALO_BLK, upper_off)
    return jnp.stack([jnp.zeros((BLOCKS,), jnp.int32), lower_off, upper_off], axis=1)


def levels(stream_key, extent, shards, low, top_value):
    def one(axis_at, shards_of):
        draws = jax.random.uniform(jax.random.fold_in(jax.random.fold_in(stream_key, 6), axis_at), (shards_of,), jnp.float32, low / len(shards), top_value / len(shards))
        return jnp.repeat(jnp.exp(draws), extent[axis_at] // shards_of).reshape((-1,) + (1,) * (len(extent) - axis_at - 1))

    level = one(*shards[0])
    for cut in shards[1:]:
        level = level * one(*cut)
    return level


def scatter_about(own_key, extent, spread, most, cuts=(), held_as=jnp.bfloat16):
    entries = spread * jax.random.normal(own_key, extent, jnp.float32)
    if cuts:
        entries = entries * levels(own_key, extent, cuts, -0.22, 0.18)
    return jnp.clip(entries, -most, most).astype(held_as)


def setup_inputs(seed: int = 0) -> dict:
    arg_keys = jax.random.split(jax.random.key(seed), 9)
    return {
        "feats": scatter_about(arg_keys[0], (NODES, D), 1.0, 6.0, ((0, 32),)),
        "tile_vals": scatter_about(arg_keys[1], (BLOCKS, TPR, BLK, BLK), (TPR * BLK) ** -0.5, 0.3125, ((0, 32),)),
        "tile_offs": draw_tile_offs(jax.random.fold_in(arg_keys[8], 71), 0),
        "w_in": scatter_about(arg_keys[3], (LAYERS, 2 * D, HID), (2 * D) ** -0.5, 0.375),
        "bias_in": scatter_about(arg_keys[4], (LAYERS, HID), 0.5, 3.0, (), jnp.float32),
        "w_out": scatter_about(arg_keys[5], (LAYERS, HID, D), HID ** -0.5, 0.5),
        "gain": jnp.clip(1.0 + 0.18 * jax.random.normal(arg_keys[6], (LAYERS, D), jnp.float32), 0.1, 1.9),
        "cot": scatter_about(arg_keys[7], (NODES, D), 1.0, 6.0, ((0, 32),)),
    }


def block_order(block_count):
    groups = N_BAND * N_REP
    return jnp.arange(block_count, dtype=jnp.int32).reshape(groups, block_count // groups)

def aggregate(feats_now, tile_vals, tile_offs):
    block_count = tile_vals.shape[0]
    tile_width = tile_vals.shape[2]
    feat_width = feats_now.shape[1]
    blocks = feats_now.reshape(block_count, tile_width, feat_width)

    def one_group(group_rows):
        columns = (group_rows[:, None] + tile_offs[group_rows]) % block_count
        pieces = blocks[columns].astype(jnp.float32)
        weights = tile_vals[group_rows].astype(jnp.float32)
        return jnp.einsum('bkij,bkjd->bid', weights, pieces).astype(jnp.bfloat16)
    result = lax.map(one_group, block_order(block_count))
    return result.reshape(-1, feat_width)

def spread_back(grad_agg, tile_vals, tile_offs):
    block_count = tile_vals.shape[0]
    tile_width = tile_vals.shape[2]
    feat_width = grad_agg.shape[1]
    grad_blocks = grad_agg.reshape(block_count, tile_width, feat_width)

    def add_group(running, group_rows):
        columns = (group_rows[:, None] + tile_offs[group_rows]) % block_count
        weights = tile_vals[group_rows].astype(jnp.float32)
        contrib = jnp.einsum('bkij,bid->bkjd', weights, grad_blocks[group_rows].astype(jnp.float32))
        running = running.at[columns.reshape(-1)].add(contrib.reshape(-1, tile_width, feat_width))
        return (running, None)
    initial = jnp.zeros((block_count, tile_width, feat_width), jnp.float32)
    running, unused = lax.scan(add_group, initial, block_order(block_count))
    return running.reshape(-1, feat_width)

def layer_forward(feats_now, agg_now, weight_in, bias_now, weight_out, gain_now):
    joined = jnp.concatenate([feats_now, agg_now], axis=1)
    pre_act = jnp.dot(joined, weight_in, preferred_element_type=jnp.float32) + bias_now
    act_now = jax.nn.silu(pre_act).astype(jnp.bfloat16)
    mixed = jnp.dot(act_now, weight_out, preferred_element_type=jnp.float32)
    centred = mixed - lax.optimization_barrier(jnp.mean(mixed, axis=1, keepdims=True))
    inv_std = lax.rsqrt(lax.optimization_barrier(jnp.mean(centred * centred, axis=1, keepdims=True)) + 1e-05)
    normed = centred * inv_std
    feats_next = (feats_now.astype(jnp.float32) + normed * gain_now).astype(jnp.bfloat16)
    return (feats_next, (joined, pre_act, act_now, normed, inv_std))

def layer_backward(grad_now, saved, weight_in, weight_out, gain_now):
    joined, pre_act, act_now, normed, inv_std = saved
    feat_width = gain_now.shape[0]
    grad_gain = lax.optimization_barrier(jnp.sum(grad_now * normed, axis=0))
    grad_norm = grad_now * gain_now
    grad_mix = inv_std * (grad_norm - lax.optimization_barrier(jnp.mean(grad_norm, axis=1, keepdims=True)) - normed * lax.optimization_barrier(jnp.mean(grad_norm * normed, axis=1, keepdims=True)))
    grad_mix_b = grad_mix.astype(jnp.bfloat16)
    grad_wout = lax.dot_general(act_now, grad_mix_b, (((0,), (0,)), ((), ())), preferred_element_type=jnp.float32)
    grad_act = lax.dot_general(grad_mix_b, weight_out, (((1,), (1,)), ((), ())), preferred_element_type=jnp.float32)
    sigma = jax.nn.sigmoid(pre_act)
    grad_pre = grad_act * sigma * (1.0 + pre_act * (1.0 - sigma))
    grad_bias = lax.optimization_barrier(jnp.sum(grad_pre, axis=0))
    grad_pre_b = grad_pre.astype(jnp.bfloat16)
    grad_win = lax.dot_general(joined, grad_pre_b, (((0,), (0,)), ((), ())), preferred_element_type=jnp.float32)
    grad_cat = lax.dot_general(grad_pre_b, weight_in, (((1,), (1,)), ((), ())), preferred_element_type=jnp.float32)
    grad_next = grad_now + grad_cat[:, :feat_width]
    grad_agg = grad_cat[:, feat_width:].astype(jnp.bfloat16)
    return (grad_next, grad_agg, grad_win, grad_bias, grad_wout, grad_gain)

def reference(feats, tile_vals, tile_offs, w_in, bias_in, w_out, gain, cot):
    feats_now = feats
    stored = []
    for layer_idx in range(LAYERS):
        agg_now = aggregate(feats_now, tile_vals, tile_offs)
        feats_now, saved = layer_forward(feats_now, agg_now, w_in[layer_idx], bias_in[layer_idx], w_out[layer_idx], gain[layer_idx])
        stored.append(saved)
    grad_now = cot.astype(jnp.float32)
    win_list, bias_list, wout_list, gain_list = ([], [], [], [])
    for layer_idx in reversed(range(LAYERS)):
        grad_now, grad_agg, grad_win, grad_bias, grad_wout, grad_gain = layer_backward(grad_now, stored[layer_idx], w_in[layer_idx], w_out[layer_idx], gain[layer_idx])
        grad_now = grad_now + spread_back(grad_agg, tile_vals, tile_offs)
        win_list.insert(0, grad_win)
        bias_list.insert(0, grad_bias)
        wout_list.insert(0, grad_wout)
        gain_list.insert(0, grad_gain)
    scale_factor = 1.0 / math.sqrt(NODES)
    return (feats_now, grad_now, jnp.stack(win_list) * scale_factor, jnp.stack(bias_list) * scale_factor, jnp.stack(wout_list) * scale_factor, jnp.stack(gain_list) * scale_factor)
```

```python
import math

import jax
import jax.numpy as jnp
from jax import lax
from jax.experimental import pallas as pl
from jax.experimental.pallas import tpu as pltpu
from jax.sharding import PartitionSpec as P

HALO = 16
EPS = 1e-05
AXES = ("band", "rep")
F32 = jnp.float32
BF16 = jnp.bfloat16
CH = 4
ANY = pl.BlockSpec(memory_space=pl.ANY)
SMEM = pl.BlockSpec(memory_space=pltpu.SMEM)
VMEM = pl.BlockSpec(memory_space=pltpu.VMEM)


def nt(a, b):
    return lax.dot_general(a, b, (((1,), (1,)), ((), ())), preferred_element_type=F32)


def nn(a, b):
    return jnp.dot(a, b, preferred_element_type=F32)


def eye(n):
    rows = lax.broadcasted_iota(jnp.int32, (n, n), 0)
    cols = lax.broadcasted_iota(jnp.int32, (n, n), 1)
    return (rows == cols).astype(BF16)


def column(row, width):
    return jnp.transpose(jnp.broadcast_to(row, (width, row.shape[1])))


def lanes(parts):
    return jnp.concatenate(parts, axis=1)


def widen(block, times):
    return lanes([block] * times)


def sigmoid(v):
    return 0.5 + 0.5 * jnp.tanh(0.5 * v)


def parity():
    place = lax.axis_index("band") * lax.axis_size("rep") + lax.axis_index("rep")
    return lax.rem(place, 2)


def start_all(copies):
    for c in copies:
        c.start()


def wait_all(copies):
    for c in copies:
        c.wait()


def swap(x, far):
    n = lax.axis_size("band") * lax.axis_size("rep")
    pairs = []
    for c in range(n // 2):
        a, b = (2 * c, 2 * c + 1) if not far else (2 * c + 1, (2 * c + 2) % n)
        pairs += [(a, b), (b, a)]
    return lax.ppermute(x, AXES, pairs)


def routed(even, start_even, start_odd):
    @pl.when(even)
    def _():
        start_all(start_even)

    @pl.when(jnp.logical_not(even))
    def _():
        start_all(start_odd)


def inner_tiles(ext, tiles, offs, part, it, first):
    slot = jnp.where(it * CH < HALO, 2, 1)
    for s in range(CH):
        b = it * CH + s
        col = b + offs[b, slot]
        left = lanes([ext[first + b], ext[first + col]])
        right = lanes([tiles[b, 0], tiles[b, slot]])
        part[b] = nt(left, right)


def load_tiles(tiles_hbm, tiles, sem, steps):
    return [
        pltpu.make_async_copy(
            tiles_hbm.at[pl.ds(i * CH, CH)], tiles.at[pl.ds(i * CH, CH)], sem.at[i]
        )
        for i in range(steps)
    ]


def inner0_kernel(nb, offs, x_hbm, tiles_hbm, h_hbm, part_hbm, x, tiles, h, part, sem, tsem):
    steps = nb // CH
    blk = tiles.shape[2]
    get_x = pltpu.make_async_copy(x_hbm, x, sem.at[0])
    get_t = load_tiles(tiles_hbm, tiles, tsem, steps)
    get_x.start()
    start_all(get_t)
    one = eye(blk)
    get_x.wait()

    def turn(it, c):
        for s in range(CH):
            b = it * CH + s
            h[b] = nt(one, x[pl.ds(b * blk, blk)]).astype(BF16)
        return c

    lax.fori_loop(0, steps, turn, 0)
    put_h = pltpu.make_async_copy(h, h_hbm, sem.at[1])
    put_h.start()

    def step(it, c):
        pltpu.make_async_copy(
            tiles_hbm.at[pl.ds(it * CH, CH)], tiles.at[pl.ds(it * CH, CH)], tsem.at[it]
        ).wait()
        inner_tiles(h, tiles, offs, part, it, 0)
        return c

    lax.fori_loop(0, steps, step, 0)
    put_p = pltpu.make_async_copy(part, part_hbm, sem.at[2])
    put_p.start()
    put_h.wait()
    put_p.wait()


def inner1_kernel(
    nb, offs, h_hbm, tiles_hbm, cot_hbm, part_hbm, cott_hbm, h, tiles, cot, cott, part, sem, tsem
):
    steps = nb // CH
    blk = tiles.shape[2]
    get_h = pltpu.make_async_copy(h_hbm, h, sem.at[0])
    get_t = load_tiles(tiles_hbm, tiles, tsem, steps)
    get_c = pltpu.make_async_copy(cot_hbm, cot, sem.at[1])
    get_h.start()
    start_all(get_t)
    get_c.start()
    get_h.wait()

    def step(it, c):
        pltpu.make_async_copy(
            tiles_hbm.at[pl.ds(it * CH, CH)], tiles.at[pl.ds(it * CH, CH)], tsem.at[it]
        ).wait()
        inner_tiles(h, tiles, offs, part, it, 0)
        return c

    lax.fori_loop(0, steps, step, 0)
    put_p = pltpu.make_async_copy(part, part_hbm, sem.at[2])
    put_p.start()
    get_c.wait()
    one = eye(blk)

    def turn(it, c):
        for s in range(CH):
            b = it * CH + s
            cott[b] = nt(one, cot[pl.ds(b * blk, blk)]).astype(BF16)
        return c

    lax.fori_loop(0, steps, turn, 0)
    put_c = pltpu.make_async_copy(cott, cott_hbm, sem.at[3])
    put_c.start()
    put_p.wait()
    put_c.wait()


def edge_tiles(tiles_hbm, rim, sem):
    return [
        pltpu.make_async_copy(tiles_hbm.at[pl.ds(0, HALO), 1], rim.at[pl.ds(0, HALO)], sem.at[0]),
        pltpu.make_async_copy(
            tiles_hbm.at[pl.ds(HALO, HALO), 2], rim.at[pl.ds(HALO, HALO)], sem.at[1]
        ),
    ]


def edge_column(offs, it, s):
    b = it * CH + s
    return b + HALO + offs[b, jnp.where(it * CH < HALO, 1, 2)]


def forward_step(it, ext, part, rim, offs, w1t, w2t, bias, gain):
    agg = []
    for s in range(CH):
        b = it * CH + s
        agg.append((part[b] + nt(ext[edge_column(offs, it, s)], rim[b])).astype(BF16))
    agg = lanes(agg)
    feats = lanes([ext[HALO + it * CH + s] for s in range(CH)])
    joined = jnp.concatenate([feats, agg], axis=0)
    pre = nn(w1t, joined) + widen(bias[...], CH)
    sig = sigmoid(pre)
    act = (pre * sig).astype(BF16)
    mix = nn(w2t, act)
    centred = mix - jnp.mean(mix, axis=0, keepdims=True)
    inv = lax.rsqrt(jnp.mean(centred * centred, axis=0, keepdims=True) + EPS)
    xhat = centred * inv
    after = (feats.astype(F32) + xhat * widen(gain[...], CH)).astype(BF16)
    return agg, pre, sig, act, xhat, inv, after


def backward_step(grad, xhat, inv, slope, w1, w2, gain):
    gx = grad * widen(gain[...], CH)
    gmix = inv * (
        gx
        - jnp.mean(gx, axis=0, keepdims=True)
        - xhat * jnp.mean(gx * xhat, axis=0, keepdims=True)
    )
    gmix = gmix.astype(BF16)
    gpre = nn(w2, gmix) * slope
    gpre_b = gpre.astype(BF16)
    gcat = nn(w1, gpre_b)
    width = grad.shape[0]
    return gmix, gpre, gpre_b, gcat[:width], gcat[width:].astype(BF16)


def cut(wide, s, blk):
    return wide[:, s * blk : (s + 1) * blk]


def fold(wide, blk):
    total = cut(wide, 0, blk)
    for s in range(1, CH):
        total = total + cut(wide, s, blk)
    return total


def push_edge(it, gagg, acc, rim, offs, blk):
    for s in range(CH):
        col = edge_column(offs, it, s)
        acc[col] += nn(cut(gagg, s, blk), rim[it * CH + s])


def outgoing(acc, send, nb, near_hbm, far_hbm, sem):
    for b in range(HALO):
        send[b] = acc[b].astype(BF16)
        send[HALO + b] = acc[HALO + nb + b].astype(BF16)
    send_rims(send, 0, HALO, near_hbm, far_hbm, sem)


def send_rims(buf, low, high, near_hbm, far_hbm, sem):
    even = parity() == 0
    lo, hi = buf.at[pl.ds(low, HALO)], buf.at[pl.ds(high, HALO)]
    routed(
        even,
        [
            pltpu.make_async_copy(lo, far_hbm, sem.at[0]),
            pltpu.make_async_copy(hi, near_hbm, sem.at[1]),
        ],
        [
            pltpu.make_async_copy(hi, far_hbm, sem.at[0]),
            pltpu.make_async_copy(lo, near_hbm, sem.at[1]),
        ],
    )
    pltpu.make_async_copy(lo, far_hbm, sem.at[0]).wait()
    pltpu.make_async_copy(hi, near_hbm, sem.at[1]).wait()


def fetch_rims(near_hbm, far_hbm, lo, hi, sem):
    routed(
        parity() == 0,
        [
            pltpu.make_async_copy(far_hbm, lo, sem.at[0]),
            pltpu.make_async_copy(near_hbm, hi, sem.at[1]),
        ],
        [
            pltpu.make_async_copy(near_hbm, lo, sem.at[0]),
            pltpu.make_async_copy(far_hbm, hi, sem.at[1]),
        ],
    )
    return [
        pltpu.make_async_copy(near_hbm, lo, sem.at[0]),
        pltpu.make_async_copy(far_hbm, hi, sem.at[1]),
    ]


def node0_kernel(
    nb, offs, near, far, h_hbm, part_hbm, tiles_hbm, w1t, w2t, bias, gain,
    near_out, far_out, h1_hbm, agg_hbm, act_hbm, slope_hbm, xhat_hbm, inv_hbm,
    halo, ext, part, rim, h1, agg, act, slope, xhat, inv, bcol, gcol, insem, outsem, edgesem,
):
    blk = rim.shape[1]
    steps = nb // CH
    rows = HALO * blk
    get = fetch_rims(near, far, halo.at[pl.ds(0, rows)], halo.at[pl.ds(rows, rows)], insem)
    get_h = pltpu.make_async_copy(h_hbm, ext.at[pl.ds(HALO, nb)], insem.at[2])
    get_p = pltpu.make_async_copy(part_hbm, part, insem.at[3])
    get_t = edge_tiles(tiles_hbm, rim, edgesem)
    start_all([get_h, get_p, *get_t])
    one = eye(blk)
    bcol[...] = column(bias[...], blk)
    gcol[...] = column(gain[...], blk)
    wait_all(get)

    def turn(it, c):
        for s in range(CH):
            b = it * CH + s
            ext[b] = nt(one, halo[pl.ds(b * blk, blk)]).astype(BF16)
            ext[HALO + nb + b] = nt(one, halo[pl.ds(rows + b * blk, blk)]).astype(BF16)
        return c

    lax.fori_loop(0, HALO // CH, turn, 0)
    wait_all([get_h, get_p, *get_t])

    def step(it, c):
        agg_w, pre, sig, act_w, xhat_w, inv_w, after = forward_step(
            it, ext, part, rim, offs, w1t[...], w2t[...], bcol, gcol
        )
        slope_w = (sig * (1.0 + pre * (1.0 - sig))).astype(BF16)
        xhat_b = xhat_w.astype(BF16)
        for s in range(CH):
            b = it * CH + s
            agg[b] = cut(agg_w, s, blk)
            act[b] = cut(act_w, s, blk)
            slope[b] = cut(slope_w, s, blk)
            xhat[b] = cut(xhat_b, s, blk)
            inv[b] = cut(inv_w, s, blk)
            h1[b] = cut(after, s, blk)
        return c

    lax.fori_loop(0, steps, step, 0)
    puts = [
        pltpu.make_async_copy(v, v_hbm, outsem.at[2 + i])
        for i, (v, v_hbm) in enumerate(
            [(h1, h1_hbm), (agg, agg_hbm), (act, act_hbm), (slope, slope_hbm), (xhat, xhat_hbm), (inv, inv_hbm)]
        )
    ]
    start_all(puts)
    send_rims(h1, 0, nb - HALO, near_out, far_out, outsem)
    wait_all(puts)


def node1_kernel(
    nb, offs, near, far, h_hbm, part_hbm, tiles_hbm, cott_hbm, w1t, w2t, w1, w2, bias, gain,
    near_out, far_out, h2_hbm, agg_hbm, act_hbm, gmix_hbm, gpre_hbm, gagg_hbm, acc_hbm, gb, gg,
    ext, part, rim, cott, h2, agg, act, gmix, gpre, gagg, acc, send, bcol, gcol, insem, outsem, edgesem,
):
    blk = rim.shape[1]
    steps = nb // CH
    get = fetch_rims(near, far, ext.at[pl.ds(0, HALO)], ext.at[pl.ds(HALO + nb, HALO)], insem)
    get_h = pltpu.make_async_copy(h_hbm, ext.at[pl.ds(HALO, nb)], insem.at[2])
    get_p = pltpu.make_async_copy(part_hbm, part, insem.at[3])
    get_c = pltpu.make_async_copy(cott_hbm, cott, insem.at[4])
    get_t = edge_tiles(tiles_hbm, rim, edgesem)
    start_all([get_h, get_p, get_c, *get_t])
    bcol[...] = column(bias[...], blk)
    gcol[...] = column(gain[...], blk)
    gb[...] = jnp.zeros_like(gb)
    gg[...] = jnp.zeros_like(gg)

    def clear(it, c):
        for s in range(CH):
            acc[it * CH + s] = jnp.zeros(acc.shape[1:], F32)
        return c

    lax.fori_loop(0, acc.shape[0] // CH, clear, 0)
    wait_all([*get, get_h, get_p, get_c, *get_t])

    def step(it, c):
        agg_w, pre, sig, act_w, xhat, inv, after = forward_step(
            it, ext, part, rim, offs, w1t[...], w2t[...], bcol, gcol
        )
        slope = sig * (1.0 + pre * (1.0 - sig))
        grad = lanes([cott[it * CH + s] for s in range(CH)]).astype(F32)
        gg[...] += fold(grad * xhat, blk)
        gmix_w, gpre_f, gpre_w, gh, gagg_w = backward_step(
            grad, xhat, inv, slope, w1[...], w2[...], gcol
        )
        gb[...] += fold(gpre_f, blk)
        rest = grad + gh
        for s in range(CH):
            b = it * CH + s
            agg[b] = cut(agg_w, s, blk)
            act[b] = cut(act_w, s, blk)
            h2[b] = cut(after, s, blk)
            gmix[b] = cut(gmix_w, s, blk)
            gpre[b] = cut(gpre_w, s, blk)
            gagg[b] = cut(gagg_w, s, blk)
            acc[HALO + b] += cut(rest, s, blk)
        push_edge(it, gagg_w, acc, rim, offs, blk)
        return c

    lax.fori_loop(0, steps, step, 0)
    puts = [
        pltpu.make_async_copy(v, v_hbm, outsem.at[2 + i])
        for i, (v, v_hbm) in enumerate(
            [(h2, h2_hbm), (agg, agg_hbm), (act, act_hbm), (gmix, gmix_hbm), (gpre, gpre_hbm),
             (gagg, gagg_hbm), (acc.at[pl.ds(HALO, nb)], acc_hbm)]
        )
    ]
    start_all(puts)
    outgoing(acc, send, nb, near_out, far_out, outsem)
    wait_all(puts)


def node2_kernel(
    nb, offs, near, far, acc_in, tiles_hbm, slope_hbm, xhat_hbm, inv_hbm, w1, w2, gain,
    near_out, far_out, gmix_hbm, gpre_hbm, gagg_hbm, acc_hbm, gb, gg,
    halo, before, rim, slope, xhat, inv, gmix, gpre, gagg, acc, send, gcol, insem, outsem, edgesem,
):
    blk = rim.shape[1]
    steps = nb // CH
    get = fetch_rims(near, far, halo.at[pl.ds(0, HALO)], halo.at[pl.ds(HALO, HALO)], insem)
    gets = [
        pltpu.make_async_copy(acc_in, before, insem.at[2]),
        pltpu.make_async_copy(slope_hbm, slope, insem.at[3]),
        pltpu.make_async_copy(xhat_hbm, xhat, insem.at[4]),
        pltpu.make_async_copy(inv_hbm, inv, insem.at[5]),
        *edge_tiles(tiles_hbm, rim, edgesem),
    ]
    start_all(gets)
    gcol[...] = column(gain[...], blk)
    gb[...] = jnp.zeros_like(gb)
    gg[...] = jnp.zeros_like(gg)

    def clear(it, c):
        for s in range(CH):
            acc[it * CH + s] = jnp.zeros(acc.shape[1:], F32)
        return c

    lax.fori_loop(0, acc.shape[0] // CH, clear, 0)
    wait_all([*get, *gets])

    def step(it, c):
        blocks = [it * CH + s for s in range(CH)]
        grad = lanes([before[b] + halo[b].astype(F32) for b in blocks])
        xhat_w = lanes([xhat[b] for b in blocks]).astype(F32)
        slope_w = lanes([slope[b] for b in blocks]).astype(F32)
        inv_w = lanes([inv[b] for b in blocks])
        gg[...] += fold(grad * xhat_w, blk)
        gmix_w, gpre_f, gpre_w, gh, gagg_w = backward_step(
            grad, xhat_w, inv_w, slope_w, w1[...], w2[...], gcol
        )
        gb[...] += fold(gpre_f, blk)
        rest = grad + gh
        for s, b in enumerate(blocks):
            gmix[b] = cut(gmix_w, s, blk)
            gpre[b] = cut(gpre_w, s, blk)
            gagg[b] = cut(gagg_w, s, blk)
            acc[HALO + b] += cut(rest, s, blk)
        push_edge(it, gagg_w, acc, rim, offs, blk)
        return c

    lax.fori_loop(0, steps, step, 0)
    puts = [
        pltpu.make_async_copy(v, v_hbm, outsem.at[2 + i])
        for i, (v, v_hbm) in enumerate(
            [(gmix, gmix_hbm), (gpre, gpre_hbm), (gagg, gagg_hbm), (acc.at[pl.ds(HALO, nb)], acc_hbm)]
        )
    ]
    start_all(puts)
    outgoing(acc, send, nb, near_out, far_out, outsem)
    wait_all(puts)


def weights_kernel(
    nb, with_out, *refs
):
    if with_out:
        (offs, gagg_hbm, acc_in, tiles_hbm, h_hbm, agg_hbm, act_hbm, gmix_hbm, gpre_hbm, gb, gg, h2_hbm,
         acc_hbm, gw, gv, out_hbm,
         gagg, acc, tiles, h, agg, act, gmix, gpre, h2, out, insem, tsem) = refs
    else:
        (offs, gagg_hbm, acc_in, tiles_hbm, h_hbm, agg_hbm, act_hbm, gmix_hbm, gpre_hbm, gb, gg,
         acc_hbm, gw, gv,
         gagg, acc, tiles, h, agg, act, gmix, gpre, insem, tsem) = refs
    blk = tiles.shape[2]
    width = h.shape[1]
    steps = nb // CH
    first = [
        pltpu.make_async_copy(gagg_hbm, gagg, insem.at[0]),
        pltpu.make_async_copy(acc_in, acc, insem.at[1]),
    ]
    then = [
        pltpu.make_async_copy(src, dst, insem.at[2 + i])
        for i, (src, dst) in enumerate(
            [(h_hbm, h), (agg_hbm, agg), (act_hbm, act), (gmix_hbm, gmix), (gpre_hbm, gpre)]
        )
    ]
    start_all(first)
    start_all(load_tiles(tiles_hbm, tiles, tsem, steps))
    start_all(then)
    if with_out:
        get_h2 = pltpu.make_async_copy(h2_hbm, h2, insem.at[7])
        get_h2.start()
    gv[0:1] = jnp.sum(jnp.transpose(gb[...]), axis=0, keepdims=True)
    gv[1:2] = jnp.sum(jnp.transpose(gg[...]), axis=0, keepdims=True)
    gw[...] = jnp.zeros_like(gw)
    wait_all(first)

    def push(it, c):
        pltpu.make_async_copy(
            tiles_hbm.at[pl.ds(it * CH, CH)], tiles.at[pl.ds(it * CH, CH)], tsem.at[it]
        ).wait()
        slot = jnp.where(it * CH < HALO, 2, 1)
        for s in range(CH):
            b = it * CH + s
            both = nn(gagg[b], lanes([tiles[b, 0], tiles[b, slot]]))
            acc[b] += both[:, :blk]
            acc[b + offs[b, slot]] += both[:, blk:]
        return c

    lax.fori_loop(0, steps, push, 0)
    put_a = pltpu.make_async_copy(acc, acc_hbm, insem.at[0])
    put_a.start()
    wait_all(then)

    def outer(it, c):
        blocks = [it * CH + s for s in range(CH)]
        gpre_w = lanes([gpre[b] for b in blocks])
        gw[0:width] += nt(lanes([h[b] for b in blocks]), gpre_w)
        gw[width : 2 * width] += nt(lanes([agg[b] for b in blocks]), gpre_w)
        gw[2 * width :] += nt(lanes([act[b] for b in blocks]), lanes([gmix[b] for b in blocks]))
        return c

    lax.fori_loop(0, steps, outer, 0)
    if with_out:
        get_h2.wait()
        one = eye(blk)

        def turn(it, c):
            for s in range(CH):
                b = it * CH + s
                out[pl.ds(b * blk, blk)] = nt(one, h2[b]).astype(BF16)
            return c

        lax.fori_loop(0, steps, turn, 0)
        put_o = pltpu.make_async_copy(out, out_hbm, insem.at[1])
        put_o.start()
        put_o.wait()
    put_a.wait()


def final_kernel(nb, near, far, acc_in, out_hbm, halo, acc, out, insem, outsem):
    blk = acc.shape[2]
    steps = nb // CH
    get = fetch_rims(near, far, halo.at[pl.ds(0, HALO)], halo.at[pl.ds(HALO, HALO)], insem)
    get_a = pltpu.make_async_copy(acc_in, acc, insem.at[2])
    get_a.start()
    wait_all([*get, get_a])

    def step(it, c):
        for s in range(CH):
            b = it * CH + s
            out[pl.ds(b * blk, blk)] = jnp.transpose(acc[b] + halo[b].astype(F32))
        pltpu.make_async_copy(
            out.at[pl.ds(it * CH * blk, CH * blk)],
            out_hbm.at[pl.ds(it * CH * blk, CH * blk)],
            outsem.at[it],
        ).start()
        return c

    lax.fori_loop(0, steps, step, 0)
    for i in range(steps):
        pltpu.make_async_copy(
            out.at[pl.ds(i * CH * blk, CH * blk)],
            out_hbm.at[pl.ds(i * CH * blk, CH * blk)],
            outsem.at[i],
        ).wait()


def call(body, name, specs, args, outs, out_specs, scratch, flops, moved):
    return pl.pallas_call(
        body,
        name=name,
        in_specs=specs,
        out_specs=out_specs,
        out_shape=[jax.ShapeDtypeStruct(s, t) for s, t in outs],
        scratch_shapes=scratch,
        compiler_params=pltpu.CompilerParams(vmem_limit_bytes=48 << 20),
        cost_estimate=pl.CostEstimate(flops=flops, bytes_accessed=moved, transcendentals=0),
    )(*args)


def dma(*n):
    return pltpu.SemaphoreType.DMA(n)


def per_device(feats, tile_vals, tile_offs, w_in, bias_in, w_out, gain, cot):
    import functools

    nodes, width = feats.shape
    nb, _, blk, _ = tile_vals.shape
    hid = w_out.shape[1]
    assert nb == 2 * HALO and width == blk and hid == width
    devices = lax.axis_size("band") * lax.axis_size("rep")
    steps = nb // CH
    rows = HALO * blk
    block = (width, blk)
    full = (nb, *block)
    rim = (HALO, *block)
    ext = (nb + 2 * HALO, *block)
    v = pltpu.VMEM
    tile_flops = 2 * blk * blk * width
    mlp_flops = 2 * nodes * (2 * width * hid + hid * width)
    mib = 2 * nodes * width

    w1t = jnp.swapaxes(w_in, 1, 2)
    w2t = jnp.swapaxes(w_out, 1, 2)
    odd = parity()
    far = swap(lax.dynamic_slice_in_dim(feats, odd * rows, rows), True)
    near = swap(lax.dynamic_slice_in_dim(feats, (1 - odd) * rows, rows), False)

    h0, part = call(
        functools.partial(inner0_kernel, nb), "inner0",
        [SMEM, ANY, ANY], (tile_offs, feats, tile_vals),
        [(full, BF16), (full, F32)], [ANY, ANY],
        [v((nodes, width), BF16), v(tile_vals.shape, BF16), v(full, BF16), v(full, F32), dma(3), dma(steps)],
        2 * nb * tile_flops, 7 * mib,
    )

    near, far, h1, agg0, act0, slope0, xhat0, inv0 = call(
        functools.partial(node0_kernel, nb), "node0",
        [SMEM, ANY, ANY, ANY, ANY, ANY, VMEM, VMEM, VMEM, VMEM],
        (tile_offs, near, far, h0, part, tile_vals, w1t[0], w2t[0], bias_in[0:1], gain[0:1]),
        [(rim, BF16), (rim, BF16), (full, BF16), (full, BF16), (full, BF16), (full, BF16), (full, BF16), ((nb, 1, blk), F32)],
        [ANY] * 8,
        [v((2 * rows, width), BF16), v(ext, BF16), v(full, F32), v(full, BF16)]
        + [v(full, BF16)] * 5
        + [v((nb, 1, blk), F32), v((hid, blk), F32), v(block, F32), dma(4), dma(8), dma(2)],
        nb * tile_flops + mlp_flops, 11 * mib,
    )

    near, far = swap(near, False), swap(far, True)
    part, cott = call(
        functools.partial(inner1_kernel, nb), "inner1",
        [SMEM, ANY, ANY, ANY], (tile_offs, h1, tile_vals, cot),
        [(full, F32), (full, BF16)], [ANY, ANY],
        [v(full, BF16), v(tile_vals.shape, BF16), v((nodes, width), BF16), v(full, BF16), v(full, F32), dma(4), dma(steps)],
        2 * nb * tile_flops, 8 * mib,
    )

    near, far, h2, agg1, act1, gmix1, gpre1, gagg, acc, gb1, gg1 = call(
        functools.partial(node1_kernel, nb), "node1",
        [SMEM, ANY, ANY, ANY, ANY, ANY, ANY] + [VMEM] * 6,
        (tile_offs, near, far, h1, part, tile_vals, cott, w1t[1], w2t[1], w_in[1], w_out[1], bias_in[1:2], gain[1:2]),
        [(rim, BF16), (rim, BF16)] + [(full, BF16)] * 6 + [(full, F32), (block, F32), (block, F32)],
        [ANY] * 9 + [VMEM] * 2,
        [v(ext, BF16), v(full, F32), v(full, BF16), v(full, BF16)]
        + [v(full, BF16)] * 6
        + [v(ext, F32), v(full, BF16), v(block, F32), v(block, F32), dma(5), dma(9), dma(2)],
        2 * nb * tile_flops + 2 * mlp_flops, 16 * mib,
    )

    near, far = swap(near, False), swap(far, True)
    acc, gw1, gv1, out_feats = call(
        functools.partial(weights_kernel, nb, True), "weights1",
        [SMEM] + [ANY] * 8 + [VMEM, VMEM, ANY],
        (tile_offs, gagg, acc, tile_vals, h1, agg1, act1, gmix1, gpre1, gb1, gg1, h2),
        [(full, F32), ((2 * width + hid, hid), F32), ((2, blk), F32), ((nodes, width), BF16)],
        [ANY, VMEM, VMEM, ANY],
        [v(full, BF16), v(full, F32), v(tile_vals.shape, BF16)]
        + [v(full, BF16)] * 6
        + [v((nodes, width), BF16), dma(8), dma(steps)],
        2 * nb * tile_flops + mlp_flops, 16 * mib,
    )

    near, far, gmix0, gpre0, gagg, acc, gb0, gg0 = call(
        functools.partial(node2_kernel, nb), "node2",
        [SMEM] + [ANY] * 7 + [VMEM] * 3 ,
        (tile_offs, near, far, acc, tile_vals, slope0, xhat0, inv0, w_in[0], w_out[0], gain[0:1]),
        [(rim, BF16), (rim, BF16)] + [(full, BF16)] * 3 + [(full, F32), (block, F32), (block, F32)],
        [ANY] * 6 + [VMEM] * 2,
        [v(full, BF16), v(full, F32), v(full, BF16), v(full, BF16), v(full, BF16), v((nb, 1, blk), F32)]
        + [v(full, BF16)] * 3
        + [v(ext, F32), v(full, BF16), v(block, F32), dma(6), dma(6), dma(2)],
        nb * tile_flops + mlp_flops, 14 * mib,
    )

    near, far = swap(near, False), swap(far, True)
    acc, gw0, gv0 = call(
        functools.partial(weights_kernel, nb, False), "weights0",
        [SMEM] + [ANY] * 8 + [VMEM, VMEM],
        (tile_offs, gagg, acc, tile_vals, h0, agg0, act0, gmix0, gpre0, gb0, gg0),
        [(full, F32), ((2 * width + hid, hid), F32), ((2, blk), F32)],
        [ANY, VMEM, VMEM],
        [v(full, BF16), v(full, F32), v(tile_vals.shape, BF16)] + [v(full, BF16)] * 5 + [dma(7), dma(steps)],
        2 * nb * tile_flops + mlp_flops, 14 * mib,
    )

    scale = 1.0 / math.sqrt(nodes * devices)
    big = jnp.concatenate([gw0, gw1], axis=0).reshape(devices, -1, hid)
    share = big.shape[1]
    small = jnp.concatenate([gv0, gv1, jnp.zeros((4, hid), F32)], axis=0)
    bundle = jnp.concatenate([big, jnp.broadcast_to(small, (devices, 8, hid))], axis=1).astype(BF16)
    parts = lax.all_to_all(bundle, AXES, 0, 0, tiled=True)
    sums = jnp.sum(parts.astype(F32), axis=0) * scale
    mine = jnp.broadcast_to(sums[:share].astype(BF16), (devices, share, hid))
    whole = lax.all_to_all(mine, AXES, 0, 0, tiled=True).astype(F32).reshape(2, -1, hid)
    vectors = sums[share:]

    (grad_feats,) = call(
        functools.partial(final_kernel, nb), "final",
        [ANY] * 3, (near, far, acc), [((nodes, width), F32)], [ANY],
        [v(full, BF16), v(full, F32), v((nodes, width), F32), dma(3), dma(steps)],
        nodes * width, 5 * mib,
    )
    return (
        out_feats,
        grad_feats,
        whole[:, : 2 * width],
        jnp.stack([vectors[0], vectors[2]]),
        whole[:, 2 * width :],
        jnp.stack([vectors[1], vectors[3]]),
    )


def solution(mesh):
    placed = (
        P(AXES, None),
        P(AXES, None, None, None),
        P(AXES, None),
        P(),
        P(),
        P(),
        P(),
        P(AXES, None),
    )
    return jax.shard_map(
        per_device,
        mesh=mesh,
        in_specs=placed,
        out_specs=(P(AXES, None), P(AXES, None), P(), P(), P(), P()),
        check_vma=False,
    )
```

```python
import functools
import math

import jax
import jax.numpy as jnp
from jax import lax
from jax.experimental import pallas as pl
from jax.experimental.pallas import tpu as pltpu
from jax.sharding import PartitionSpec as P

HALO = 16
EPS = 1e-05
AXES = ("band", "rep")
F32 = jnp.float32
BF16 = jnp.bfloat16
CH = 8
HBM = pl.BlockSpec(memory_space=pltpu.HBM)
ANY = pl.BlockSpec(memory_space=pl.ANY)
SMEM = pl.BlockSpec(memory_space=pltpu.SMEM)
VMEM = pl.BlockSpec(memory_space=pltpu.VMEM)


def nt(a, b):
    return lax.dot_general(a, b, (((1,), (1,)), ((), ())), preferred_element_type=F32)


def nn(a, b):
    return jnp.dot(a, b, preferred_element_type=F32)


def eye(n):
    rows = lax.broadcasted_iota(jnp.int32, (n, n), 0)
    cols = lax.broadcasted_iota(jnp.int32, (n, n), 1)
    return (rows == cols).astype(BF16)


def column(row, width):
    return jnp.transpose(jnp.broadcast_to(row, (width, row.shape[1])))


def lanes(parts):
    return jnp.concatenate(parts, axis=1)


def widen(block, times):
    return lanes([block] * times)


def parity():
    place = lax.axis_index("band") * lax.axis_size("rep") + lax.axis_index("rep")
    return lax.rem(place, 2)


def swap(x, far):
    n = lax.axis_size("band") * lax.axis_size("rep")
    pairs = []
    for c in range(n // 2):
        a, b = (2 * c, 2 * c + 1) if not far else (2 * c + 1, (2 * c + 2) % n)
        pairs += [(a, b), (b, a)]
    return lax.ppermute(x, AXES, pairs)


def by_side(near, far, move):
    even = parity() == 0

    @pl.when(even)
    def _():
        move(far, near)

    @pl.when(jnp.logical_not(even))
    def _():
        move(near, far)


def for_blocks(count, body, per=4):
    def step(it, c):
        for s in range(per):
            body(it * per + s)
        return c

    lax.fori_loop(0, count // per, step, 0)


def turn_kernel(nb, x_hbm, ext, near, far, x, sem):
    blk = ext.shape[2]
    one = eye(blk)
    parts = sem.shape[0]
    per = nb // parts

    def copy(i):
        rows = pl.ds(i * per * blk, per * blk)
        return pltpu.make_async_copy(x_hbm.at[rows], x.at[rows], sem.at[i])

    for i in range(parts):
        copy(i).start()

    def step(i, c):
        copy(i).wait()
        for s in range(per):
            b = i * per + s
            ext[HALO + b] = nt(one, x[pl.ds(b * blk, blk)]).astype(BF16)
        return c

    lax.fori_loop(0, parts, step, 0)
    give_rims(ext, HALO, nb, near, far)


def give_rims(buf, first, nb, near, far):
    def move(low, high):
        def one(b):
            low[b] = buf[first + b].astype(BF16)
            high[b] = buf[first + nb - HALO + b].astype(BF16)

        for_blocks(HALO, one)

    by_side(near, far, move)


def give_sums(acc, nb, near, far):
    def move(low, high):
        def one(b):
            low[b] = acc[b].astype(BF16)
            high[b] = acc[HALO + nb + b].astype(BF16)

        for_blocks(HALO, one)

    by_side(near, far, move)


def send_rims(rims, near_hbm, far_hbm, sem):
    low, high = rims.at[pl.ds(0, HALO)], rims.at[pl.ds(HALO, HALO)]

    def move(to_low, to_high):
        pltpu.make_async_copy(low, to_low, sem.at[0]).start()
        pltpu.make_async_copy(high, to_high, sem.at[1]).start()

    by_side(near_hbm, far_hbm, move)
    return [
        pltpu.make_async_copy(low, far_hbm, sem.at[0]),
        pltpu.make_async_copy(high, near_hbm, sem.at[1]),
    ]


def fetch_rims(near_hbm, far_hbm, rims, sem):
    low, high = rims.at[pl.ds(0, HALO)], rims.at[pl.ds(HALO, HALO)]

    def move(from_low, from_high):
        pltpu.make_async_copy(from_low, low, sem.at[0]).start()
        pltpu.make_async_copy(from_high, high, sem.at[1]).start()

    by_side(near_hbm, far_hbm, move)
    return [
        pltpu.make_async_copy(far_hbm, low, sem.at[0]),
        pltpu.make_async_copy(near_hbm, high, sem.at[1]),
    ]


def take_rims(near, far, buf, low_at, high_at):
    def move(low, high):
        def one(b):
            buf[low_at + b] = low[b]
            buf[high_at + b] = high[b]

        for_blocks(HALO, one)

    by_side(near, far, move)


def inner_tiles(nb, ext, tiles, offs, part):
    def one(b):
        slot = jnp.where(b < HALO, 2, 1)
        left = lanes([ext[HALO + b], ext[HALO + b + offs[slot, b]]])
        part[b] = nt(left, lanes([tiles[b, 0], tiles[b, slot]]))

    for_blocks(nb, one)


def inner0_kernel(nb, offs, ext, tiles, w_in, w_out, part, w1t, w2t, w2, kept, sem):
    keep = pltpu.make_async_copy(ext.at[pl.ds(HALO, nb)], kept, sem.at[0])
    keep.start()
    inner_tiles(nb, ext, tiles, offs, part)
    one = eye(tiles.shape[2])
    for layer in range(w_in.shape[0]):
        w1t[layer] = (0.5 * nt(one, w_in[layer])).astype(BF16)
        w2t[layer] = nt(one, w_out[layer]).astype(BF16)
        w2[layer] = (0.5 * w_out[layer].astype(F32)).astype(BF16)
    keep.wait()


def inner1_kernel(nb, offs, ext, tiles, cot, part, cott):
    inner_tiles(nb, ext, tiles, offs, part)
    blk = tiles.shape[2]
    one = eye(blk)

    def turn(b):
        cott[b] = nt(one, cot[pl.ds(b * blk, blk)]).astype(BF16)

    for_blocks(nb, turn)


def edge_slot(b):
    return jnp.where(b < HALO, 1, 2)


def forward_step(it, ext, part, tiles, offs, w1t, w2t, bias, gain):
    agg = []
    for s in range(CH):
        b = it * CH + s
        slot = edge_slot(b)
        agg.append((part[b] + nt(ext[HALO + b + offs[slot, b]], tiles[b, slot])).astype(BF16))
    agg = lanes(agg)
    feats = lanes([ext[HALO + it * CH + s] for s in range(CH)])
    joined = jnp.concatenate([feats, agg], axis=0)
    half = nn(w1t, joined) + widen(bias[...], CH)
    t = jnp.tanh(half)
    up = 1.0 + t
    act = (half * up).astype(BF16)
    slope = up * (1.0 + half * (1.0 - t))
    mix = nn(w2t, act)
    centred = mix - jnp.mean(mix, axis=0, keepdims=True)
    inv = lax.rsqrt(jnp.mean(centred * centred, axis=0, keepdims=True) + EPS)
    xhat = centred * inv
    after = (feats.astype(F32) + xhat * widen(gain[...], CH)).astype(BF16)
    return agg, act, slope, xhat, inv, after


def backward_step(grad, xhat, inv, slope, w1, w2, gain):
    wide = widen(gain[...], CH)
    prod = grad * xhat
    gx = grad * wide
    gmix = inv * (
        gx - jnp.mean(gx, axis=0, keepdims=True) - xhat * jnp.mean(prod * wide, axis=0, keepdims=True)
    )
    gmix = gmix.astype(BF16)
    gpre = nn(w2, gmix) * slope
    gpre_b = gpre.astype(BF16)
    gcat = nn(w1, gpre_b)
    width = grad.shape[0]
    return prod, gmix, gpre, gpre_b, gcat[:width], gcat[width:].astype(BF16)


def cut(wide, s, blk):
    return wide[:, s * blk : (s + 1) * blk]


def fold(wide, blk):
    total = cut(wide, 0, blk)
    for s in range(1, CH):
        total = total + cut(wide, s, blk)
    return total


def push_edge(it, gagg, acc, tiles, offs, blk):
    for s in range(CH):
        b = it * CH + s
        slot = edge_slot(b)
        acc[HALO + b + offs[slot, b]] += nn(cut(gagg, s, blk), tiles[b, slot])


def push_inner(b, gagg, acc, first, tiles, offs, blk):
    slot = jnp.where(b < HALO, 2, 1)
    both = nn(gagg[b], lanes([tiles[b, 0], tiles[b, slot]]))
    acc[first + b] += both[:, :blk]
    acc[first + b + offs[slot, b]] += both[:, blk:]


def clear(ref):
    def one(b):
        ref[b] = jnp.zeros(ref.shape[1:], ref.dtype)

    for_blocks(ref.shape[0], one)


def node0_kernel(
    nb, offs, near, far, ext_in, part, tiles, w1t, w2t, bias, gain,
    near_out, far_out, ext, after_ext, agg, act, slope, xhat, inv, bcol, gcol,
):
    blk = tiles.shape[2]
    bcol[...] = column(0.5 * bias[0:1], blk)
    gcol[...] = column(gain[0:1], blk)
    take_rims(near, far, ext, 0, HALO + nb)

    def step(it, c):
        agg_w, act_w, slope_w, xhat_w, inv_w, after = forward_step(
            it, ext, part, tiles, offs, w1t[0], w2t[0], bcol, gcol
        )
        slope_w = slope_w.astype(BF16)
        xhat_b = xhat_w.astype(BF16)
        for s in range(CH):
            b = it * CH + s
            agg[b] = cut(agg_w, s, blk)
            act[b] = cut(act_w, s, blk)
            slope[b] = cut(slope_w, s, blk)
            xhat[b] = cut(xhat_b, s, blk)
            inv[b] = cut(inv_w, s, blk)
            after_ext[HALO + b] = cut(after, s, blk)
        return c

    lax.fori_loop(0, nb // CH, step, 0)
    give_rims(after_ext, HALO, nb, near_out, far_out)


def node1_kernel(
    nb, offs, near, far, ext_in, part, tiles, cott, w1t, w2t, w_in, w2, bias, gain,
    near_out, far_out, ext, h2, agg, act, gmix, gpre, gagg, acc, gb, gg, bcol, gcol,
):
    blk = tiles.shape[2]
    bcol[...] = column(0.5 * bias[1:2], blk)
    gcol[...] = column(gain[1:2], blk)
    gb[...] = jnp.zeros_like(gb)
    gg[...] = jnp.zeros_like(gg)
    clear(acc)
    take_rims(near, far, ext, 0, HALO + nb)

    def step(it, c):
        agg_w, act_w, slope, xhat, inv, after = forward_step(
            it, ext, part, tiles, offs, w1t[1], w2t[1], bcol, gcol
        )
        grad = lanes([cott[it * CH + s] for s in range(CH)]).astype(F32)
        prod, gmix_w, gpre_f, gpre_w, gh, gagg_w = backward_step(
            grad, xhat, inv, slope, w_in[1], w2[1], gcol
        )
        gg[...] += fold(prod, blk)
        gb[...] += fold(gpre_f, blk)
        rest = grad + gh
        for s in range(CH):
            b = it * CH + s
            agg[b] = cut(agg_w, s, blk)
            act[b] = cut(act_w, s, blk)
            h2[b] = cut(after, s, blk)
            gmix[b] = cut(gmix_w, s, blk)
            gpre[b] = cut(gpre_w, s, blk)
            gagg[b] = cut(gagg_w, s, blk)
            acc[HALO + b] += cut(rest, s, blk)
        push_edge(it, gagg_w, acc, tiles, offs, blk)
        return c

    lax.fori_loop(0, nb // CH, step, 0)
    give_sums(acc, nb, near_out, far_out)


def outer_step(blocks, feats, first, agg, act, gmix, gpre, gw):
    width = feats.shape[1]
    gpre_w = lanes([gpre[b] for b in blocks])
    gw[0:width] += nt(lanes([feats[first + b] for b in blocks]), gpre_w)
    gw[width : 2 * width] += nt(lanes([agg[b] for b in blocks]), gpre_w)
    gw[2 * width :] += nt(lanes([act[b] for b in blocks]), lanes([gmix[b] for b in blocks]))


def row_sum(block):
    return jnp.sum(jnp.transpose(block), axis=0, keepdims=True)


def weights_kernel(
    nb, offs, gagg, acc_in, tiles, ext, agg, act, gmix, gpre, gb, gg, h2, acc, gw, gv, out_hbm, out, sem,
):
    blk = tiles.shape[2]
    one = eye(blk)

    def turn(b):
        out[pl.ds(b * blk, blk)] = nt(one, h2[b]).astype(BF16)

    for_blocks(nb, turn)
    put = pltpu.make_async_copy(out, out_hbm, sem.at[0])
    put.start()
    gv[0:1] = row_sum(gb[...])
    gv[1:2] = row_sum(gg[...])
    for_blocks(nb, lambda b: push_inner(b, gagg, acc, HALO, tiles, offs, blk))
    gw[...] = jnp.zeros_like(gw)

    def outer(it, c):
        outer_step([it * CH + s for s in range(CH)], ext, HALO, agg, act, gmix, gpre, gw)
        return c

    lax.fori_loop(0, nb // CH, outer, 0)
    put.wait()


def node2_kernel(
    nb, offs, near, far, acc_in, tiles, slope, xhat, inv, w_in, w2, gain, kept, agg, act, gw1, gv1,
    near_hbm, far_hbm, bundle_hbm, gagg_hbm, acc_hbm,
    gagg, acc, halo, gmix, gpre, gb, gg, gw, gcol, bundle, sem,
):
    blk = tiles.shape[2]
    gcol[...] = column(gain[0:1], blk)
    gb[...] = jnp.zeros_like(gb)
    gg[...] = jnp.zeros_like(gg)
    gw[...] = jnp.zeros_like(gw)
    clear(acc)
    take_rims(near, far, halo, 0, HALO)

    def step(it, c):
        blocks = [it * CH + s for s in range(CH)]
        grad = lanes([acc_in[HALO + b] + halo[b].astype(F32) for b in blocks])
        xhat_w = lanes([xhat[b] for b in blocks]).astype(F32)
        slope_w = lanes([slope[b] for b in blocks]).astype(F32)
        inv_w = lanes([inv[b] for b in blocks])
        prod, gmix_w, gpre_f, gpre_w, gh, gagg_w = backward_step(
            grad, xhat_w, inv_w, slope_w, w_in[0], w2[0], gcol
        )
        gg[...] += fold(prod, blk)
        gb[...] += fold(gpre_f, blk)
        rest = grad + gh
        for s, b in enumerate(blocks):
            gmix[b] = cut(gmix_w, s, blk)
            gpre[b] = cut(gpre_w, s, blk)
            gagg[b] = cut(gagg_w, s, blk)
            acc[HALO + b] += cut(rest, s, blk)
        some = pl.ds(it * CH, CH)
        pltpu.make_async_copy(gagg.at[some], gagg_hbm.at[some], sem.at[1]).start()
        push_edge(it, gagg_w, acc, tiles, offs, blk)
        outer_step(blocks, kept, 0, agg, act, gmix, gpre, gw)
        return c

    lax.fori_loop(0, nb // CH, step, 0)
    put = pltpu.make_async_copy(acc.at[pl.ds(HALO, nb)], acc_hbm, sem.at[0])
    put.start()

    def rim_sum(b):
        halo[b] = acc[b].astype(BF16)
        halo[HALO + b] = acc[HALO + nb + b].astype(BF16)

    for_blocks(HALO, rim_sum)
    sent = send_rims(halo, near_hbm, far_hbm, sem.at[pl.ds(2, 2)])
    devices = bundle.shape[0]
    rows = gw.shape[0]
    share = 2 * rows // devices
    vectors = jnp.concatenate([row_sum(gb[...]), row_sum(gg[...]), gv1[...]], axis=0)
    vectors = jnp.concatenate([vectors, jnp.zeros_like(vectors)], axis=0).astype(BF16)
    for p in range(devices):
        bundle[p, 0:8] = vectors
        at = p * share
        if at + share <= rows:
            mine = gw[at : at + share]
        elif at >= rows:
            mine = gw1[at - rows : at - rows + share]
        else:
            mine = jnp.concatenate([gw[at:rows], gw1[0 : at + share - rows]], axis=0)
        bundle[p, 8 : 8 + share] = mine.astype(BF16)
    out = pltpu.make_async_copy(bundle, bundle_hbm, sem.at[4])
    out.start()
    pltpu.make_async_copy(gagg, gagg_hbm, sem.at[1]).wait()
    for c in [*sent, put, out]:
        c.wait()


def total_kernel(scale, parts, mine_hbm, gbias, ggain, mine, sem):
    total = jnp.sum(parts[...].astype(F32), axis=0) * scale
    mine[...] = jnp.broadcast_to(total[8:][None], mine.shape).astype(BF16)
    put = pltpu.make_async_copy(mine, mine_hbm, sem.at[0])
    put.start()
    gbias[0:1] = total[0:1]
    ggain[0:1] = total[1:2]
    gbias[1:2] = total[2:3]
    ggain[1:2] = total[3:4]
    put.wait()


def final_kernel(
    nb, offs, near, far, acc_hbm, gagg_hbm, tiles_hbm, out_hbm, acc, gagg, tiles, halo, out, sem, tsem
):
    blk = tiles.shape[2]
    per = nb // tsem.shape[0]
    get_a = pltpu.make_async_copy(acc_hbm, acc, sem.at[0])
    get_g = pltpu.make_async_copy(gagg_hbm, gagg, sem.at[1])

    def get_t(it):
        some = pl.ds(it * per, per)
        return pltpu.make_async_copy(tiles_hbm.at[some], tiles.at[some], tsem.at[it])

    get_g.start()
    get_a.start()
    for it in range(nb // per):
        get_t(it).start()
    rims = fetch_rims(near, far, halo, sem.at[pl.ds(2, 2)])
    get_g.wait()
    get_a.wait()

    def push(it, c):
        get_t(it).wait()
        for s in range(per):
            push_inner(it * per + s, gagg, acc, 0, tiles, offs, blk)
        return c

    lax.fori_loop(0, nb // per, push, 0)

    for c in rims:
        c.wait()

    def put(it):
        rows = pl.ds(it * per * blk, per * blk)
        return pltpu.make_async_copy(out.at[rows], out_hbm.at[rows], tsem.at[it])

    def step(it, c):
        for s in range(per):
            b = it * per + s
            out[pl.ds(b * blk, blk)] = jnp.transpose(acc[b] + halo[b].astype(F32))
        put(it).start()
        return c

    lax.fori_loop(0, nb // per, step, 0)
    for it in range(nb // per):
        put(it).wait()


def unpack_kernel(sums, out1_hbm, out2_hbm, out1, out2, sem):
    devices, share, _ = sums.shape
    layers, upper, _ = out1.shape
    rows = upper + out2.shape[1]
    for p in range(devices):
        mine = sums[p].astype(F32)
        at = p * share
        while at < (p + 1) * share:
            layer, row = divmod(at, rows)
            end = min((p + 1) * share, layer * rows + (upper if row < upper else rows))
            piece = mine[at - p * share : end - p * share]
            if row < upper:
                out1[layer, row : row + end - at] = piece
            else:
                out2[layer, row - upper : row - upper + end - at] = piece
            at = end
    puts = [
        pltpu.make_async_copy(out1, out1_hbm, sem.at[0]),
        pltpu.make_async_copy(out2, out2_hbm, sem.at[1]),
    ]
    for p in puts:
        p.start()
    for p in puts:
        p.wait()


def call(
    body, name, args, outs, scratch=(), alias=None, far_args=(), any_args=(), flops=0, moved=0
):
    args = [
        pltpu.with_memory_space_constraint(a, pltpu.HBM) if i in far_args else a
        for i, a in enumerate(args)
    ]
    return pl.pallas_call(
        body,
        name=name,
        in_specs=[
            HBM if i in far_args else ANY if i in any_args else SMEM if a.dtype == jnp.int32 else VMEM
            for i, a in enumerate(args)
        ],
        out_specs=[HBM if len(o) == 3 else VMEM for o in outs],
        out_shape=[
            pltpu.HBM(o[0], o[1]) if len(o) == 3 else jax.ShapeDtypeStruct(o[0], o[1]) for o in outs
        ],
        scratch_shapes=list(scratch),
        input_output_aliases=alias or {},
        compiler_params=pltpu.CompilerParams(vmem_limit_bytes=24 << 20),
        cost_estimate=pl.CostEstimate(flops=flops, bytes_accessed=moved, transcendentals=0),
    )(*args)


def dma(n):
    return pltpu.SemaphoreType.DMA((n,))


def per_device(feats, tile_vals, tile_offs, w_in, bias_in, w_out, gain, cot):
    nodes, width = feats.shape
    nb, slots, blk, _ = tile_vals.shape
    hid = w_out.shape[1]
    layers = w_in.shape[0]
    assert nb == 2 * HALO and width == blk and hid == width and layers == 2
    devices = lax.axis_size("band") * lax.axis_size("rep")
    block = (width, blk)
    full, rim, ext = ((n, *block) for n in (nb, HALO, nb + 2 * HALO))
    whole = (2 * width + hid, hid)
    share = layers * whole[0] // devices
    assert share * devices == layers * whole[0]
    rims = [(rim, BF16), (rim, BF16)]
    v = pltpu.VMEM
    part_of = functools.partial
    tile_flops = 2 * blk * blk * width
    mlp_flops = 2 * nodes * (2 * width * hid + hid * width)
    mib = 2 * nodes * width
    offs = tile_offs.T

    h0, near, far = call(
        part_of(turn_kernel, nb), "turn", (feats,), [(ext, BF16), *rims],
        [v((nodes, width), BF16), dma(4)], far_args=(0,),
        flops=nb * tile_flops, moved=3 * mib,
    )
    near, far = swap(near, False), swap(far, True)
    part, w1t, w2t, w2, kept = call(
        part_of(inner0_kernel, nb), "inner0", (offs, h0, tile_vals, w_in, w_out),
        [(full, F32), ((layers, hid, 2 * width), BF16), ((layers, width, hid), BF16), (w_out.shape, BF16), (full, BF16, True)],
        [dma(1)],
        flops=2 * nb * tile_flops, moved=6 * mib,
    )
    near, far, h0, h1, agg0, act0, slope0, xhat0, inv0 = call(
        part_of(node0_kernel, nb), "node0",
        (offs, near, far, h0, part, tile_vals, w1t, w2t, bias_in, gain),
        [*rims, (ext, BF16), (ext, BF16), (full, BF16), (full, BF16), (full, BF16), (full, BF16), ((nb, 1, blk), F32)],
        [v(block, F32), v(block, F32)], {3: 2},
        flops=nb * tile_flops + mlp_flops, moved=11 * mib,
    )
    near, far = swap(near, False), swap(far, True)
    part, cott = call(
        part_of(inner1_kernel, nb), "inner1", (offs, h1, tile_vals, cot), [(full, F32), (full, BF16)],
        flops=2 * nb * tile_flops, moved=8 * mib,
    )
    near, far, h1, h2, agg1, act1, gmix1, gpre1, gagg, acc, gb1, gg1 = call(
        part_of(node1_kernel, nb), "node1",
        (offs, near, far, h1, part, tile_vals, cott, w1t, w2t, w_in, w2, bias_in, gain),
        [*rims, (ext, BF16), *[(full, BF16)] * 6, (ext, F32), (block, F32), (block, F32)],
        [v(block, F32), v(block, F32)], {3: 2},
        flops=2 * nb * tile_flops + 2 * mlp_flops, moved=16 * mib,
    )
    near, far = swap(near, False), swap(far, True)
    acc, gw1, gv1, out_feats = call(
        part_of(weights_kernel, nb), "weights1",
        (offs, gagg, acc, tile_vals, h1, agg1, act1, gmix1, gpre1, gb1, gg1, h2),
        [(ext, F32), (whole, F32), ((2, hid), F32), ((nodes, width), BF16, True)],
        [v((nodes, width), BF16), dma(1)], {2: 0},
        flops=2 * nb * tile_flops + mlp_flops, moved=16 * mib,
    )
    near, far, bundle, gagg, acc = call(
        part_of(node2_kernel, nb), "node2",
        (offs, near, far, acc, tile_vals, slope0, xhat0, inv0, w_in, w2, gain, kept, agg0, act0, gw1, gv1),
        [(rim, BF16, True), (rim, BF16, True), ((devices, 8 + share, hid), BF16, True), (full, BF16, True), (full, F32, True)],
        [v(full, BF16), v(ext, F32), v(full, BF16), v(full, BF16), v(full, BF16)]
        + [v(block, F32), v(block, F32), v(whole, F32), v(block, F32), v((devices, 8 + share, hid), BF16), dma(5)],
        flops=nb * tile_flops + 2 * mlp_flops, moved=14 * mib,
    )

    parts = lax.all_to_all(bundle, AXES, 0, 0, tiled=True)
    near, far = swap(near, False), swap(far, True)
    mine, grad_bias, grad_gain = call(
        part_of(total_kernel, 1.0 / math.sqrt(nodes * devices)), "total", (parts,),
        [((devices, share, hid), BF16, True), ((layers, hid), F32), ((layers, width), F32)],
        [v((devices, share, hid), BF16), dma(1)],
        flops=nodes * width, moved=mib,
    )
    sums = lax.all_to_all(mine, AXES, 0, 0, tiled=True)
    (grad_feats,) = call(
        part_of(final_kernel, nb), "final", (offs, near, far, acc, gagg, tile_vals),
        [((nodes, width), F32, True)],
        [v(full, F32), v(full, BF16), v((nb, slots, blk, blk), BF16), v(full, BF16), v((nodes, width), F32), dma(4), dma(8)],
        far_args=(3, 4, 5), any_args=(1, 2),
        flops=2 * nb * tile_flops, moved=9 * mib,
    )
    grad_w_in, grad_w_out = call(
        unpack_kernel, "unpack", (sums,),
        [((layers, 2 * width, hid), F32, True), ((layers, hid, width), F32, True)],
        [v((layers, 2 * width, hid), F32), v((layers, hid, width), F32), dma(2)],
        flops=nodes * width, moved=mib,
    )
    return out_feats, grad_feats, grad_w_in, grad_bias, grad_w_out, grad_gain


def solution(mesh):
    placed = (
        P(AXES, None),
        P(AXES, None, None, None),
        P(AXES, None),
        P(),
        P(),
        P(),
        P(),
        P(AXES, None),
    )
    return jax.shard_map(
        per_device,
        mesh=mesh,
        in_specs=placed,
        out_specs=(P(AXES, None), P(AXES, None), P(), P(), P(), P()),
        check_vma=False,
    )
```

```python
import functools
import math

import jax
import jax.numpy as jnp
from jax import lax
from jax.experimental import pallas as pl
from jax.experimental.pallas import tpu as pltpu
from jax.sharding import PartitionSpec as P


HALO = 16
EPS = 1e-05
AXES = ("band", "rep")
F32 = jnp.float32
BF16 = jnp.bfloat16
CH = 8
HBM = pl.BlockSpec(memory_space=pltpu.HBM)
ANY = pl.BlockSpec(memory_space=pl.ANY)
SMEM = pl.BlockSpec(memory_space=pltpu.SMEM)
VMEM = pl.BlockSpec(memory_space=pltpu.VMEM)


def nt(a, b):
    return lax.dot_general(a, b, (((1,), (1,)), ((), ())), preferred_element_type=F32)


def nn(a, b):
    return jnp.dot(a, b, preferred_element_type=F32)


def eye(n):
    rows = lax.broadcasted_iota(jnp.int32, (n, n), 0)
    cols = lax.broadcasted_iota(jnp.int32, (n, n), 1)
    return (rows == cols).astype(BF16)


def column(row, width):
    return jnp.transpose(jnp.broadcast_to(row, (width, row.shape[1])))


def lanes(parts):
    return jnp.concatenate(parts, axis=1)


def widen(block, times):
    return lanes([block] * times)


def parity():
    place = lax.axis_index("band") * lax.axis_size("rep") + lax.axis_index("rep")
    return lax.rem(place, 2)


def swap(x, far):
    n = lax.axis_size("band") * lax.axis_size("rep")
    pairs = []
    for c in range(n // 2):
        a, b = (2 * c, 2 * c + 1) if not far else (2 * c + 1, (2 * c + 2) % n)
        pairs += [(a, b), (b, a)]
    return lax.ppermute(x, AXES, pairs)


def rim_at(nb, far):
    odd = parity()
    return (odd if far else 1 - odd) * (HALO + nb)


def rows_at(far):
    odd = parity()
    return (odd if far else 1 - odd) * HALO


def for_blocks(count, body, per=4):
    def step(it, c):
        for s in range(per):
            body(it * per + s)
        return c

    lax.fori_loop(0, count // per, step, 0)


def turn_rows(x, ext, out, base, one):
    blk = ext.shape[2]

    def turn(b):
        block = nt(one, x[pl.ds(b * blk, blk)]).astype(BF16)
        ext[HALO + base + b] = block
        out[b] = block

    for_blocks(HALO, turn, 8)


def half_of(x_hbm, x, base, sem):
    rows = x.shape[0]
    return pltpu.make_async_copy(
        x_hbm.at[pl.ds(pl.multiple_of(base * (rows // HALO), rows), rows)], x, sem
    )


def turn_kernel(x_hbm, ext, far, x, sem):
    base = rows_at(True)
    get = half_of(x_hbm, x, base, sem.at[0])
    get.start()
    one = eye(ext.shape[2])
    get.wait()
    turn_rows(x, ext, far, base, one)


def fetch_rims(near_hbm, far_hbm, rims, sem):
    copies = [
        pltpu.make_async_copy(far_hbm, rims.at[pl.ds(rows_at(True), HALO)], sem.at[0]),
        pltpu.make_async_copy(near_hbm, rims.at[pl.ds(rows_at(False), HALO)], sem.at[1]),
    ]
    for c in copies:
        c.start()
    return copies


def take_rim(rim, buf, at):
    def one(b):
        buf[at + b] = rim[b]

    for_blocks(HALO, one, 8)


def inner_tile(b, ext, tiles, offs, part):
    slot = jnp.where(b < HALO, 2, 1)
    left = lanes([ext[HALO + b], ext[HALO + b + offs[slot, b]]])
    part[b] = nt(left, lanes([tiles[b, 0], tiles[b, slot]]))


def inner0_kernel(
    nb, offs, ext_in, x_hbm, tiles_hbm, w_in_hbm, w_out_hbm,
    ext, near, part, w1t, w2t, w2, kept, x, tiles, w_in, w_out, sem, tsem,
):
    base = rows_at(False)
    per = nb // tsem.shape[0]

    def get_t(it):
        some = pl.ds(it * per, per)
        return pltpu.make_async_copy(tiles_hbm.at[some], tiles.at[some], tsem.at[it])

    get = half_of(x_hbm, x, base, sem.at[1])
    gets = [
        pltpu.make_async_copy(w_in_hbm, w_in, sem.at[2]),
        pltpu.make_async_copy(w_out_hbm, w_out, sem.at[3]),
    ]
    get.start()
    for it in range(nb // per):
        get_t(it).start()
    for c in gets:
        c.start()
    one = eye(tiles.shape[2])
    get.wait()
    turn_rows(x, ext, near, base, one)
    keep = pltpu.make_async_copy(ext.at[pl.ds(HALO, nb)], kept, sem.at[0])
    keep.start()

    def step(it, c):
        get_t(it).wait()
        for s in range(per):
            inner_tile(it * per + s, ext, tiles, offs, part)
        return c

    lax.fori_loop(0, nb // per, step, 0)
    for c in gets:
        c.wait()
    for layer in range(w_in.shape[0]):
        w1t[layer] = (0.5 * nt(one, w_in[layer])).astype(BF16)
        w2t[layer] = nt(one, w_out[layer]).astype(BF16)
        w2[layer] = (0.5 * w_out[layer].astype(F32)).astype(BF16)
    keep.wait()


def inner1_kernel(nb, offs, ext, tiles, cot, part, cott):
    for_blocks(nb, lambda b: inner_tile(b, ext, tiles, offs, part))
    blk = tiles.shape[2]
    one = eye(blk)

    def turn(b):
        cott[b] = nt(one, cot[pl.ds(b * blk, blk)]).astype(BF16)

    for_blocks(nb, turn)


def edge_slot(b):
    return jnp.where(b < HALO, 1, 2)


def forward_step(blocks, ext, part, tiles, offs, w1t, w2t, bias, gain):
    agg = []
    for b in blocks:
        slot = edge_slot(b)
        agg.append((part[b] + nt(ext[HALO + b + offs[slot, b]], tiles[b, slot])).astype(BF16))
    agg = lanes(agg)
    feats = lanes([ext[HALO + b] for b in blocks])
    joined = jnp.concatenate([feats, agg], axis=0)
    half = nn(w1t, joined) + widen(bias[...], CH)
    t = jnp.tanh(half)
    up = 1.0 + t
    act = (half * up).astype(BF16)
    slope = up * (1.0 + half * (1.0 - t))
    mix = nn(w2t, act)
    centred = mix - jnp.mean(mix, axis=0, keepdims=True)
    inv = lax.rsqrt(jnp.mean(centred * centred, axis=0, keepdims=True) + EPS)
    xhat = centred * inv
    after = (feats.astype(F32) + xhat * widen(gain[...], CH)).astype(BF16)
    return agg, act, slope, xhat, inv, after


def backward_step(grad, xhat, inv, slope, w1, w2, gain):
    wide = widen(gain[...], CH)
    prod = grad * xhat
    gx = grad * wide
    gmix = inv * (
        gx - jnp.mean(gx, axis=0, keepdims=True) - xhat * jnp.mean(prod * wide, axis=0, keepdims=True)
    )
    gmix = gmix.astype(BF16)
    gpre = nn(w2, gmix) * slope
    gpre_b = gpre.astype(BF16)
    gcat = nn(w1, gpre_b)
    width = grad.shape[0]
    return prod, gmix, gpre, gpre_b, gcat[:width], gcat[width:].astype(BF16)


def cut(wide, s, blk):
    return wide[:, s * blk : (s + 1) * blk]


def fold(wide, blk):
    total = cut(wide, 0, blk)
    for s in range(1, CH):
        total = total + cut(wide, s, blk)
    return total


def push_edge(blocks, gagg, acc, tiles, offs, blk):
    for s, b in enumerate(blocks):
        slot = edge_slot(b)
        acc[HALO + b + offs[slot, b]] += nn(cut(gagg, s, blk), tiles[b, slot])


def push_inner(b, gagg, acc, first, tiles, offs, blk):
    slot = jnp.where(b < HALO, 2, 1)
    both = nn(gagg, lanes([tiles[b, 0], tiles[b, slot]]))
    acc[first + b] += both[:, :blk]
    acc[first + b + offs[slot, b]] += both[:, blk:]


def clear(ref):
    def one(b):
        ref[b] = jnp.zeros(ref.shape[1:], ref.dtype)

    for_blocks(ref.shape[0], one)


def node0_kernel(
    nb, is_far, offs, rim, ext_in, part, tiles, w1t, w2t, bias, gain, *refs
):
    rim_out, ext, after_ext, agg, act, slope, xhat, inv, bcol, gcol = refs if is_far else refs[1:]
    blk = tiles.shape[2]
    bcol[...] = column(0.5 * bias[0:1], blk)
    gcol[...] = column(gain[0:1], blk)
    take_rim(rim, ext, rim_at(nb, is_far))
    base = rows_at(is_far)

    def step(it, c):
        local = [it * CH + s for s in range(CH)]
        agg_w, act_w, slope_w, xhat_w, inv_w, after = forward_step(
            [base + b for b in local], ext, part, tiles, offs, w1t[0], w2t[0], bcol, gcol
        )
        slope_w = slope_w.astype(BF16)
        xhat_b = xhat_w.astype(BF16)
        for s, b in enumerate(local):
            agg[b] = cut(agg_w, s, blk)
            act[b] = cut(act_w, s, blk)
            slope[b] = cut(slope_w, s, blk)
            xhat[b] = cut(xhat_b, s, blk)
            inv[b] = cut(inv_w, s, blk)
            after_ext[HALO + base + b] = cut(after, s, blk)
            rim_out[b] = cut(after, s, blk)
        return c

    lax.fori_loop(0, HALO // CH, step, 0)


def node1_kernel(
    nb, is_far, offs, rim, ext_in, part, tiles, cott, w1t, w2t, w_in, w2, bias, gain, *refs
):
    rim_out, ext, h2, agg, act, gmix, gpre, gagg, acc, gb, gg, bcol, gcol = refs if is_far else refs[3:]
    blk = tiles.shape[2]
    bcol[...] = column(0.5 * bias[1:2], blk)
    gcol[...] = column(gain[1:2], blk)
    if is_far:
        gb[...] = jnp.zeros_like(gb)
        gg[...] = jnp.zeros_like(gg)
        clear(acc)
    take_rim(rim, ext, rim_at(nb, is_far))
    base = rows_at(is_far)

    def step(it, c):
        local = [it * CH + s for s in range(CH)]
        blocks = [base + b for b in local]
        agg_w, act_w, slope, xhat, inv, after = forward_step(
            blocks, ext, part, tiles, offs, w1t[1], w2t[1], bcol, gcol
        )
        grad = lanes([cott[b] for b in blocks]).astype(F32)
        prod, gmix_w, gpre_f, gpre_w, gh, gagg_w = backward_step(
            grad, xhat, inv, slope, w_in[1], w2[1], gcol
        )
        gg[...] += fold(prod, blk)
        gb[...] += fold(gpre_f, blk)
        rest = grad + gh
        for s, b in enumerate(local):
            agg[b] = cut(agg_w, s, blk)
            act[b] = cut(act_w, s, blk)
            h2[b] = cut(after, s, blk)
            gmix[b] = cut(gmix_w, s, blk)
            gpre[b] = cut(gpre_w, s, blk)
            gagg[b] = cut(gagg_w, s, blk)
            acc[HALO + base + b] += cut(rest, s, blk)
        push_edge(blocks, gagg_w, acc, tiles, offs, blk)
        return c

    lax.fori_loop(0, HALO // CH, step, 0)
    at = rim_at(nb, is_far)

    def give(b):
        rim_out[b] = acc[at + b].astype(BF16)

    for_blocks(HALO, give, 8)


def outer_step(local, feats, first, agg, act, gmix, gpre, gw):
    width = feats.shape[1]
    gpre_w = lanes([gpre[b] for b in local])
    gw[0:width] += nt(lanes([feats[first + b] for b in local]), gpre_w)
    gw[width : 2 * width] += nt(lanes([agg[b] for b in local]), gpre_w)
    gw[2 * width :] += nt(lanes([act[b] for b in local]), lanes([gmix[b] for b in local]))


def row_sum(block):
    return jnp.sum(jnp.transpose(block), axis=0, keepdims=True)


def weights_kernel(offs, acc_in, tiles, ext, gb, gg, *refs):
    halves, (acc, gw, gv, h2_hbm, sem) = (refs[:6], refs[6:12]), refs[12:]
    blk = tiles.shape[2]
    puts = [
        pltpu.make_async_copy(half[0], h2_hbm.at[pl.ds(rows_at(is_far), HALO)], sem.at[i])
        for i, (is_far, half) in enumerate(zip((True, False), halves))
    ]
    for c in puts:
        c.start()
    gv[0:1] = row_sum(gb[...])
    gv[1:2] = row_sum(gg[...])
    gw[...] = jnp.zeros_like(gw)
    for is_far, (_, agg, act, gmix, gpre, gagg) in zip((True, False), halves):
        base = rows_at(is_far)
        for_blocks(HALO, lambda b: push_inner(base + b, gagg[b], acc, HALO, tiles, offs, blk))

        def outer(it, c):
            local = [it * CH + s for s in range(CH)]
            outer_step(local, ext, HALO + base, agg, act, gmix, gpre, gw)
            return c

        lax.fori_loop(0, HALO // CH, outer, 0)
    for c in puts:
        c.wait()


def output_kernel(nb, h_hbm, out_hbm, h, out, sem):
    blk = h.shape[2]
    per = nb // sem.shape[0]

    def get(it):
        some = pl.ds(it * per, per)
        return pltpu.make_async_copy(h_hbm.at[some], h.at[some], sem.at[it])

    def put(it):
        rows = pl.ds(pl.multiple_of(it * per * blk, per * blk), per * blk)
        return pltpu.make_async_copy(out.at[rows], out_hbm.at[rows], sem.at[it])

    for it in range(nb // per):
        get(it).start()
    one = eye(blk)

    def step(it, c):
        get(it).wait()
        for s in range(per):
            b = it * per + s
            out[pl.ds(pl.multiple_of(b * blk, blk), blk)] = nt(one, h[b]).astype(BF16)
        put(it).start()
        return c

    lax.fori_loop(0, nb // per, step, 0)
    for it in range(nb // per):
        put(it).wait()


def node2_kernel(nb, is_far, offs, rim, acc_in, tiles, w_in, w2, gain, kept, agg, act, slope, xhat, inv, *refs):
    if is_far:
        (near_in, gw1, gv1, *_, near_hbm, far_hbm, bundle_hbm, gagg_hbm, acc_hbm,
         acc, gb, gg, gw, gagg, gmix, gpre, gcol, rims, bundle, sem) = refs
    else:
        acc, gb, gg, gw, gagg_hbm, near_sum, gagg, gmix, gpre, gcol, sem = refs
    blk = tiles.shape[2]
    gcol[...] = column(gain[0:1], blk)
    if is_far:
        pass
    else:
        gb[...] = jnp.zeros_like(gb)
        gg[...] = jnp.zeros_like(gg)
        gw[...] = jnp.zeros_like(gw)
        clear(acc)
    base = rows_at(is_far)

    def step(it, c):
        local = [it * CH + s for s in range(CH)]
        blocks = [base + b for b in local]
        grad = lanes([acc_in[HALO + base + b] + rim[b].astype(F32) for b in local])
        xhat_w = lanes([xhat[b] for b in local]).astype(F32)
        slope_w = lanes([slope[b] for b in local]).astype(F32)
        inv_w = lanes([inv[b] for b in local])
        prod, gmix_w, gpre_f, gpre_w, gh, gagg_w = backward_step(
            grad, xhat_w, inv_w, slope_w, w_in[0], w2[0], gcol
        )
        gg[...] += fold(prod, blk)
        gb[...] += fold(gpre_f, blk)
        rest = grad + gh
        for s, b in enumerate(local):
            gmix[b] = cut(gmix_w, s, blk)
            gpre[b] = cut(gpre_w, s, blk)
            gagg[b] = cut(gagg_w, s, blk)
            acc[HALO + base + b] += cut(rest, s, blk)
        some = pl.ds(it * CH, CH)
        pltpu.make_async_copy(gagg.at[some], gagg_hbm.at[some], sem.at[1]).start()
        push_edge(blocks, gagg_w, acc, tiles, offs, blk)
        outer_step(local, kept, base, agg, act, gmix, gpre, gw)
        return c

    lax.fori_loop(0, HALO // CH, step, 0)
    at = rim_at(nb, is_far)
    if not is_far:

        def give(b):
            near_sum[b] = acc[at + b].astype(BF16)

        for_blocks(HALO, give, 8)
        pltpu.make_async_copy(gagg, gagg_hbm, sem.at[1]).wait()
        return
    put = pltpu.make_async_copy(acc.at[pl.ds(HALO, nb)], acc_hbm, sem.at[0])
    put.start()

    def rim_sum(b):
        rims[b] = acc[at + b].astype(BF16)

    for_blocks(HALO, rim_sum, 8)
    sent = [
        pltpu.make_async_copy(rims, far_hbm, sem.at[2]),
        pltpu.make_async_copy(near_in, near_hbm, sem.at[3]),
    ]
    for c in sent:
        c.start()
    devices = bundle.shape[0]
    rows = gw.shape[0]
    share = 2 * rows // devices
    vectors = jnp.concatenate([row_sum(gb[...]), row_sum(gg[...]), gv1[...]], axis=0)
    vectors = jnp.concatenate([vectors, jnp.zeros_like(vectors)], axis=0).astype(BF16)
    for p in range(devices):
        bundle[p, 0:8] = vectors
        first = p * share
        if first + share <= rows:
            mine = gw[first : first + share]
        elif first >= rows:
            mine = gw1[first - rows : first - rows + share]
        else:
            mine = jnp.concatenate([gw[first:rows], gw1[0 : first + share - rows]], axis=0)
        bundle[p, 8 : 8 + share] = mine.astype(BF16)
    out = pltpu.make_async_copy(bundle, bundle_hbm, sem.at[4])
    out.start()
    pltpu.make_async_copy(gagg, gagg_hbm, sem.at[1]).wait()
    for c in [*sent, put, out]:
        c.wait()


def total_kernel(scale, parts, mine_hbm, gbias, ggain, mine, sem):
    total = jnp.sum(parts[...].astype(F32), axis=0) * scale
    mine[...] = jnp.broadcast_to(total[8:][None], mine.shape).astype(BF16)
    put = pltpu.make_async_copy(mine, mine_hbm, sem.at[0])
    put.start()
    gbias[0:1] = total[0:1]
    ggain[0:1] = total[1:2]
    gbias[1:2] = total[2:3]
    ggain[1:2] = total[3:4]
    put.wait()


def final_kernel(
    nb, offs, near, far, acc_hbm, gagg_far, gagg_near, tiles_hbm, out_hbm,
    acc, gagg, tiles, halo, out, sem, tsem,
):
    blk = tiles.shape[2]
    per = nb // tsem.shape[0]
    get_a = pltpu.make_async_copy(acc_hbm, acc, sem.at[0])

    def get_t(it):
        some = pl.ds(it * per, per)
        return pltpu.make_async_copy(tiles_hbm.at[some], tiles.at[some], tsem.at[it])

    get_g = fetch_rims(gagg_near, gagg_far, gagg, sem.at[pl.ds(4, 2)])
    get_a.start()
    for it in range(nb // per):
        get_t(it).start()
    rims = fetch_rims(near, far, halo, sem.at[pl.ds(2, 2)])
    for c in get_g:
        c.wait()
    get_a.wait()

    def push(it, c):
        get_t(it).wait()
        for s in range(per):
            push_inner(it * per + s, gagg[it * per + s], acc, 0, tiles, offs, blk)
        return c

    lax.fori_loop(0, nb // per, push, 0)

    for c in rims:
        c.wait()

    def put(it):
        rows = pl.ds(it * per * blk, per * blk)
        return pltpu.make_async_copy(out.at[rows], out_hbm.at[rows], tsem.at[it])

    def step(it, c):
        for s in range(per):
            b = it * per + s
            out[pl.ds(b * blk, blk)] = jnp.transpose(acc[b] + halo[b].astype(F32))
        put(it).start()
        return c

    lax.fori_loop(0, nb // per, step, 0)
    for it in range(nb // per):
        put(it).wait()


def unpack_kernel(sums, out1_hbm, out2_hbm, out1, out2, sem):
    devices, share, _ = sums.shape
    _, upper, _ = out1.shape
    rows = upper + out2.shape[1]
    for p in range(devices):
        mine = sums[p].astype(F32)
        at = p * share
        while at < (p + 1) * share:
            layer, row = divmod(at, rows)
            end = min((p + 1) * share, layer * rows + (upper if row < upper else rows))
            piece = mine[at - p * share : end - p * share]
            if row < upper:
                out1[layer, row : row + end - at] = piece
            else:
                out2[layer, row - upper : row - upper + end - at] = piece
            at = end
    puts = [
        pltpu.make_async_copy(out1, out1_hbm, sem.at[0]),
        pltpu.make_async_copy(out2, out2_hbm, sem.at[1]),
    ]
    for p in puts:
        p.start()
    for p in puts:
        p.wait()


def call(body, args, outs, scratch=(), alias=None, far_args=(), any_args=(), flops=0, moved=0):
    args = [
        pltpu.with_memory_space_constraint(a, pltpu.HBM) if i in far_args else a
        for i, a in enumerate(args)
    ]
    return pl.pallas_call(
        body,
        in_specs=[
            HBM if i in far_args else ANY if i in any_args else SMEM if a.dtype == jnp.int32 else VMEM
            for i, a in enumerate(args)
        ],
        out_specs=[HBM if len(o) == 3 else VMEM for o in outs],
        out_shape=[
            pltpu.HBM(o[0], o[1]) if len(o) == 3 else jax.ShapeDtypeStruct(o[0], o[1]) for o in outs
        ],
        scratch_shapes=list(scratch),
        input_output_aliases=alias or {},
        compiler_params=pltpu.CompilerParams(vmem_limit_bytes=24 << 20),
        cost_estimate=pl.CostEstimate(flops=flops, bytes_accessed=moved, transcendentals=0),
    )(*args)


def dma(n):
    return pltpu.SemaphoreType.DMA((n,))


def per_device(feats, tile_vals, tile_offs, w_in, bias_in, w_out, gain, cot):
    nodes, width = feats.shape
    nb, slots, blk, _ = tile_vals.shape
    hid = w_out.shape[1]
    layers = w_in.shape[0]
    assert nb == 2 * HALO and width == blk and hid == width and layers == 2
    devices = lax.axis_size("band") * lax.axis_size("rep")
    block = (width, blk)
    full, _, ext = ((n, *block) for n in (nb, HALO, nb + 2 * HALO))
    whole = (2 * width + hid, hid)
    share = layers * whole[0] // devices
    assert share * devices == layers * whole[0]
    v = pltpu.VMEM
    part_of = functools.partial
    tile_flops = 2 * blk * blk * width
    mlp_flops = 2 * nodes * (2 * width * hid + hid * width)
    mib = 2 * nodes * width
    offs = tile_offs.T

    half = (HALO, *block)
    half_rows = (nodes // 2, width)

    h0, far = call(
        turn_kernel, (feats,), [(ext, BF16), (half, BF16)],
        [v(half_rows, BF16), dma(1)], far_args=(0,),
        flops=nb * tile_flops, moved=3 * mib,
    )
    far = swap(far, True)
    h0, near, part, w1t, w2t, w2, kept = call(
        part_of(inner0_kernel, nb), (offs, h0, feats, tile_vals, w_in, w_out),
        [(ext, BF16), (half, BF16), (full, F32), ((layers, hid, 2 * width), BF16), ((layers, width, hid), BF16),
         (w_out.shape, BF16), (full, BF16, True)],
        [v(half_rows, BF16), v(tile_vals.shape, BF16), v(w_in.shape, BF16), v(w_out.shape, BF16), dma(4), dma(8)],
        {1: 0}, far_args=(2, 3, 4, 5),
        flops=2 * nb * tile_flops, moved=6 * mib,
    )
    near = swap(near, False)

    def node0(is_far, rim, h, more):
        return call(
            part_of(node0_kernel, nb, is_far),
            (offs, rim, h, part, tile_vals, w1t, w2t, bias_in, gain, *more),
            [(half, BF16), (ext, BF16), (ext, BF16), *[(half, BF16)] * 4, ((HALO, 1, blk), F32)],
            [v(block, F32), v(block, F32)], {2: 1} if is_far else {2: 1, 9: 2},
            flops=(nb * tile_flops + mlp_flops) // 2, moved=6 * mib,
        )

    far, h0, h1, *saved_far = node0(True, far, h0, ())
    far = swap(far, True)
    near, h0, h1, *saved_near = node0(False, near, h0, (h1,))
    near = swap(near, False)
    part, cott = call(
        part_of(inner1_kernel, nb), (offs, h1, tile_vals, cot), [(full, F32), (full, BF16)],
        flops=2 * nb * tile_flops, moved=8 * mib,
    )

    def node1(is_far, rim, h, more):
        return call(
            part_of(node1_kernel, nb, is_far),
            (offs, rim, h, part, tile_vals, cott, w1t, w2t, w_in, w2, bias_in, gain, *more),
            [(half, BF16), (ext, BF16), *[(half, BF16)] * 6, (ext, F32), (block, F32), (block, F32)],
            [v(block, F32), v(block, F32)], {2: 1} if is_far else {2: 1, 12: 8, 13: 9, 14: 10},
            flops=nb * tile_flops + mlp_flops, moved=8 * mib,
        )

    far, h1, *made_far, acc, gb1, gg1 = node1(True, far, h1, ())
    far = swap(far, True)
    near, h1, *made_near, acc, gb1, gg1 = node1(False, near, h1, (acc, gb1, gg1))
    near = swap(near, False)
    acc, gw1, gv1, h2 = call(
        weights_kernel, (offs, acc, tile_vals, h1, gb1, gg1, *made_far, *made_near),
        [(ext, F32), (whole, F32), ((2, hid), F32), (full, BF16, True)],
        [dma(2)], {1: 0},
        flops=tile_flops, moved=mib,
    )

    def node2(is_far, rim, acc, saved, more, outs, scratch, alias):
        return call(
            part_of(node2_kernel, nb, is_far),
            (offs, rim, acc, tile_vals, w_in, w2, gain, kept, *saved, *more), outs, scratch, alias,
            flops=nb * tile_flops + mlp_flops, moved=8 * mib,
        )

    sums = [(ext, F32), (block, F32), (block, F32), (whole, F32)]
    work = [v(half, BF16), v(half, BF16), v(half, BF16), v(block, F32)]
    *state, gagg_near, near = node2(
        False, near, acc, saved_near, (), [*sums, (half, BF16, True), (half, BF16)], [*work, dma(2)], {}
    )
    near, far, bundle, gagg_far, acc, *_ = node2(
        True, far, acc, saved_far, (near, gw1, gv1, *state),
        [(half, BF16, True), (half, BF16, True), ((devices, 8 + share, hid), BF16, True), (half, BF16, True), (full, F32, True), *sums],
        [*work, v(half, BF16), v((devices, 8 + share, hid), BF16), dma(5)],
        {16 + i: 5 + i for i in range(4)},
    )

    parts = lax.all_to_all(bundle, AXES, 0, 0, tiled=True)
    near, far = swap(near, False), swap(far, True)
    (out_feats,) = call(
        part_of(output_kernel, nb), (h2,), [((nodes, width), BF16, True)],
        [v(full, BF16), v((nodes, width), BF16), dma(4)], far_args=(0,),
        flops=nb * tile_flops, moved=2 * mib,
    )
    mine, grad_bias, grad_gain = call(
        part_of(total_kernel, 1.0 / math.sqrt(nodes * devices)), (parts,),
        [((devices, share, hid), BF16, True), ((layers, hid), F32), ((layers, width), F32)],
        [v((devices, share, hid), BF16), dma(1)],
        flops=nodes * width, moved=mib,
    )
    sums = lax.all_to_all(mine, AXES, 0, 0, tiled=True)
    (grad_feats,) = call(
        part_of(final_kernel, nb), (offs, near, far, acc, gagg_far, gagg_near, tile_vals),
        [((nodes, width), F32, True)],
        [v(full, F32), v(full, BF16), v((nb, slots, blk, blk), BF16), v(full, BF16), v((nodes, width), F32), dma(6), dma(8)],
        far_args=(3, 4, 5, 6), any_args=(1, 2),
        flops=2 * nb * tile_flops, moved=9 * mib,
    )
    grad_w_in, grad_w_out = call(
        unpack_kernel, (sums,),
        [((layers, 2 * width, hid), F32, True), ((layers, hid, width), F32, True)],
        [v((layers, 2 * width, hid), F32), v((layers, hid, width), F32), dma(2)],
        flops=nodes * width, moved=mib,
    )
    return out_feats, grad_feats, grad_w_in, grad_bias, grad_w_out, grad_gain


def solution(mesh):
    placed = (
        P(AXES, None),
        P(AXES, None, None, None),
        P(AXES, None),
        P(),
        P(),
        P(),
        P(),
        P(AXES, None),
    )
    return jax.shard_map(
        per_device,
        mesh=mesh,
        in_specs=placed,
        out_specs=(P(AXES, None), P(AXES, None), P(), P(), P(), P()),
        check_vma=False,
    )
```

```python
import functools
import math

import jax
import jax.numpy as jnp
from jax import lax
from jax.experimental import pallas as pl
from jax.experimental.pallas import tpu as pltpu
from jax.sharding import PartitionSpec as P


HALO = 16
EPS = 1e-05
AXES = ("band", "rep")
F32 = jnp.float32
BF16 = jnp.bfloat16
OUTER = 8
CH = 4
HBM = pl.BlockSpec(memory_space=pltpu.HBM)
ANY = pl.BlockSpec(memory_space=pl.ANY)
SMEM = pl.BlockSpec(memory_space=pltpu.SMEM)
VMEM = pl.BlockSpec(memory_space=pltpu.VMEM)


def nt(a, b):
    return lax.dot_general(a, b, (((1,), (1,)), ((), ())), preferred_element_type=F32)


def nn(a, b):
    return jnp.dot(a, b, preferred_element_type=F32)


def eye(n):
    rows = lax.broadcasted_iota(jnp.int32, (n, n), 0)
    cols = lax.broadcasted_iota(jnp.int32, (n, n), 1)
    return (rows == cols).astype(BF16)


def column(row, width):
    return jnp.transpose(jnp.broadcast_to(row, (width, row.shape[1])))


def lanes(parts):
    return jnp.concatenate(parts, axis=1)


def widen(block, times):
    return lanes([block] * times)


def parity():
    place = lax.axis_index("band") * lax.axis_size("rep") + lax.axis_index("rep")
    return lax.rem(place, 2)


def swap(x, far):
    n = lax.axis_size("band") * lax.axis_size("rep")
    pairs = []
    for c in range(n // 2):
        a, b = (2 * c, 2 * c + 1) if not far else (2 * c + 1, (2 * c + 2) % n)
        pairs += [(a, b), (b, a)]
    return lax.ppermute(x, AXES, pairs)


def rim_at(nb, far):
    odd = parity()
    return (odd if far else 1 - odd) * (HALO + nb)


def rows_at(far):
    odd = parity()
    return (odd if far else 1 - odd) * HALO


def pipelined(count, *stages):
    held = {}
    for t in range(count + len(stages) - 1):
        for i, stage in enumerate(stages):
            if 0 <= t - i < count:
                held[t - i] = stage(t - i, *held.get(t - i, ()))


def for_blocks(count, body, per=4):
    def step(it, c):
        for s in range(per):
            body(it * per + s)
        return c

    lax.fori_loop(0, count // per, step, 0)


def turn_rows(x, ext, out, base, one):
    blk = ext.shape[2]

    def turn(b):
        block = nt(one, x[pl.ds(b * blk, blk)]).astype(BF16)
        ext[HALO + base + b] = block
        out[b] = block

    for_blocks(HALO, turn, 8)


def half_of(x_hbm, x, base, sem):
    rows = x.shape[0]
    return pltpu.make_async_copy(
        x_hbm.at[pl.ds(pl.multiple_of(base * (rows // HALO), rows), rows)], x, sem
    )


def turn_kernel(x_hbm, ext, far, x, sem):
    base = rows_at(True)
    blk = ext.shape[2]
    pieces = sem.shape[0]
    per = HALO // pieces

    def get(i):
        rows = per * blk
        return pltpu.make_async_copy(
            x_hbm.at[pl.ds(pl.multiple_of((base + i * per) * blk, rows), rows)],
            x.at[pl.ds(i * rows, rows)],
            sem.at[i],
        )

    for i in range(pieces):
        get(i).start()
    one = eye(blk)
    for i in range(pieces):
        get(i).wait()
        for b in range(i * per, (i + 1) * per):
            block = nt(one, x[b * blk : (b + 1) * blk]).astype(BF16)
            ext[HALO + base + b] = block
            far[b] = block


def fetch_rims(near_hbm, far_hbm, rims, sem):
    copies = [
        pltpu.make_async_copy(far_hbm, rims.at[pl.ds(rows_at(True), HALO)], sem.at[0]),
        pltpu.make_async_copy(near_hbm, rims.at[pl.ds(rows_at(False), HALO)], sem.at[1]),
    ]
    for c in copies:
        c.start()
    return copies


def take_rim(rim, buf, at):
    def one(b):
        buf[at + b] = rim[b]

    for_blocks(HALO, one, 8)


def inner_tile(b, ext, tiles, offs, part):
    slot = jnp.where(b < HALO, 2, 1)
    left = lanes([ext[HALO + b], ext[HALO + b + offs[slot, b]]])
    part[b] = nt(left, lanes([tiles[b, 0], tiles[b, slot]]))


def inner0_kernel(
    nb, offs, ext_in, x_hbm, tiles_hbm, w_in_hbm, w_out_hbm, bias, gain,
    ext, near, part, w1t, w2t, w2, bcols, gcols, kept, x, tiles, w_in, w_out, sem, tsem,
):
    base = rows_at(False)
    per = nb // tsem.shape[0]

    def get_t(it):
        some = pl.ds(it * per, per)
        return pltpu.make_async_copy(tiles_hbm.at[some], tiles.at[some], tsem.at[it])

    get = half_of(x_hbm, x, base, sem.at[1])
    gets = [
        pltpu.make_async_copy(w_in_hbm, w_in, sem.at[2]),
        pltpu.make_async_copy(w_out_hbm, w_out, sem.at[3]),
    ]
    get.start()
    for it in range(nb // per):
        get_t(it).start()
    for c in gets:
        c.start()
    one = eye(tiles.shape[2])
    get.wait()
    turn_rows(x, ext, near, base, one)
    keep = pltpu.make_async_copy(ext.at[pl.ds(HALO, nb)], kept, sem.at[0])
    keep.start()

    def step(it, c):
        get_t(it).wait()
        for s in range(per):
            inner_tile(it * per + s, ext, tiles, offs, part)
        return c

    lax.fori_loop(0, nb // per, step, 0)
    for c in gets:
        c.wait()
    for layer in range(w_in.shape[0]):
        w1t[layer] = (0.5 * nt(one, w_in[layer])).astype(BF16)
        w2t[layer] = nt(one, w_out[layer]).astype(BF16)
        w2[layer] = (0.5 * w_out[layer].astype(F32)).astype(BF16)
        bcols[layer] = column(0.5 * bias[layer : layer + 1], bcols.shape[2])
        gcols[layer] = column(gain[layer : layer + 1], gcols.shape[2])
    keep.wait()


def inner1_kernel(nb, offs, ext, tiles, cot, part, cott, acc1, acc0):
    for_blocks(nb, lambda b: inner_tile(b, ext, tiles, offs, part))
    blk = tiles.shape[2]
    one = eye(blk)

    def turn(b):
        cott[b] = nt(one, cot[pl.ds(b * blk, blk)]).astype(BF16)

    for_blocks(nb, turn)
    clear(acc1)
    clear(acc0)


def edge_slot(b):
    return jnp.where(b < HALO, 1, 2)


def join_step(blocks, ext, part, tiles, offs, w1t, bias):
    agg = []
    for b in blocks:
        slot = edge_slot(b)
        agg.append((part[b] + nt(ext[HALO + b + offs[slot, b]], tiles[b, slot])).astype(BF16))
    agg = lanes(agg)
    feats = lanes([ext[HALO + b] for b in blocks])
    half = nn(w1t, jnp.concatenate([feats, agg], axis=0)) + widen(bias[...], CH)
    return feats, agg, half


def mix_step(half, w2t):
    t = jnp.tanh(half)
    up = 1.0 + t
    act = (half * up).astype(BF16)
    slope = up * (1.0 + half * (1.0 - t))
    return act, slope, nn(w2t, act)


def norm_step(feats, mix, gain):
    centred = mix - jnp.mean(mix, axis=0, keepdims=True)
    inv = lax.rsqrt(jnp.mean(centred * centred, axis=0, keepdims=True) + EPS)
    xhat = centred * inv
    after = (feats.astype(F32) + xhat * widen(gain[...], CH)).astype(BF16)
    return xhat, inv, after


def unmix_step(grad, xhat, inv, w2, gain):
    wide = widen(gain[...], CH)
    prod = grad * xhat
    gx = grad * wide
    gmix = inv * (
        gx - jnp.mean(gx, axis=0, keepdims=True) - xhat * jnp.mean(prod * wide, axis=0, keepdims=True)
    )
    gmix = gmix.astype(BF16)
    return prod, gmix, nn(w2, gmix)


def unjoin_step(gact, slope, w1):
    gpre = gact * slope
    gpre_b = gpre.astype(BF16)
    gcat = nn(w1, gpre_b)
    width = gact.shape[0]
    return gpre, gpre_b, gcat[:width], gcat[width:].astype(BF16)


def chunk(base, it):
    return [base + it * CH + s for s in range(CH)]


def cut(wide, s, blk):
    return wide[:, s * blk : (s + 1) * blk]


def fold(wide, blk):
    total = cut(wide, 0, blk)
    for s in range(1, CH):
        total = total + cut(wide, s, blk)
    return total


def push_edge(blocks, gagg, acc, tiles, offs, blk):
    for s, b in enumerate(blocks):
        slot = edge_slot(b)
        acc[HALO + b + offs[slot, b]] += nn(cut(gagg, s, blk), tiles[b, slot])


def push_inner(b, gagg, acc, first, tiles, offs, blk):
    slot = jnp.where(b < HALO, 2, 1)
    both = nn(gagg, lanes([tiles[b, 0], tiles[b, slot]]))
    acc[first + b] += both[:, :blk]
    acc[first + b + offs[slot, b]] += both[:, blk:]


def clear(ref):
    def one(b):
        ref[b] = jnp.zeros(ref.shape[1:], ref.dtype)

    for_blocks(ref.shape[0], one)


def node0_kernel(
    nb, is_far, offs, rim, ext_in, part, tiles, w1t, w2t, bcols, gcols, *refs
):
    rim_out, ext, after_ext, agg, act, slope, xhat, inv = refs if is_far else refs[1:]
    bcol, gcol = bcols.at[0], gcols.at[0]
    blk = tiles.shape[2]
    take_rim(rim, ext, rim_at(nb, is_far))
    base = rows_at(is_far)

    def join(it):
        return join_step(chunk(base, it), ext, part, tiles, offs, w1t[0], bcol)

    def mixing(it, feats, agg_w, half):
        for s, b in enumerate(chunk(0, it)):
            agg[b] = cut(agg_w, s, blk)
        return feats, *mix_step(half, w2t[0])

    def norm(it, feats, act_w, slope_w, mix):
        xhat_w, inv_w, after = norm_step(feats, mix, gcol)
        slope_w, xhat_w = slope_w.astype(BF16), xhat_w.astype(BF16)
        for s, b in enumerate(chunk(0, it)):
            act[b] = cut(act_w, s, blk)
            slope[b] = cut(slope_w, s, blk)
            xhat[b] = cut(xhat_w, s, blk)
            inv[b] = cut(inv_w, s, blk)
            after_ext[HALO + base + b] = cut(after, s, blk)
            rim_out[b] = cut(after, s, blk)

    pipelined(HALO // CH, join, mixing, norm)


def node1_kernel(
    nb, is_far, offs, rim, ext_in, part, tiles, cott, w1t, w2t, w_in, w2, bcols, gcols, *refs
):
    rim_out, ext, h2, agg, act, gmix, gpre, gagg, acc, gb, gg = refs[1:] if is_far else refs[3:]
    bcol, gcol = bcols.at[1], gcols.at[1]
    blk = tiles.shape[2]
    if is_far:
        gb[...] = jnp.zeros_like(gb)
        gg[...] = jnp.zeros_like(gg)
    take_rim(rim, ext, rim_at(nb, is_far))
    base = rows_at(is_far)

    def join(it):
        return join_step(chunk(base, it), ext, part, tiles, offs, w1t[1], bcol)

    def mixing(it, feats, agg_w, half):
        for s, b in enumerate(chunk(0, it)):
            agg[b] = cut(agg_w, s, blk)
        return feats, *mix_step(half, w2t[1])

    def turn(it, feats, act_w, slope, mix):
        xhat, inv, after = norm_step(feats, mix, gcol)
        grad = lanes([cott[b] for b in chunk(base, it)]).astype(F32)
        prod, gmix_w, gact = unmix_step(grad, xhat, inv, w2[1], gcol)
        gg[...] += fold(prod, blk)
        for s, b in enumerate(chunk(0, it)):
            act[b] = cut(act_w, s, blk)
            h2[b] = cut(after, s, blk)
            gmix[b] = cut(gmix_w, s, blk)
        return slope, gact

    def unjoin(it, slope, gact):
        gpre_f, gpre_w, gh, gagg_w = unjoin_step(gact, slope, w_in[1])
        gb[...] += fold(gpre_f, blk)
        grad = lanes([cott[b] for b in chunk(base, it)]).astype(F32)
        return gpre_w, grad + gh, gagg_w

    def push(it, gpre_w, rest, gagg_w):
        for s, b in enumerate(chunk(0, it)):
            gpre[b] = cut(gpre_w, s, blk)
            gagg[b] = cut(gagg_w, s, blk)
            acc[HALO + base + b] += cut(rest, s, blk)
        push_edge(chunk(base, it), gagg_w, acc, tiles, offs, blk)

    pipelined(HALO // CH, join, mixing, turn, unjoin, push)
    at = rim_at(nb, is_far)

    def give(b):
        rim_out[b] = acc[at + b].astype(BF16)

    for_blocks(HALO, give, 8)


def outer_step(local, feats, first, agg, act, gmix, gpre, gw):
    width = feats.shape[1]
    gpre_w = lanes([gpre[b] for b in local])
    gw[0:width] += nt(lanes([feats[first + b] for b in local]), gpre_w)
    gw[width : 2 * width] += nt(lanes([agg[b] for b in local]), gpre_w)
    gw[2 * width :] += nt(lanes([act[b] for b in local]), lanes([gmix[b] for b in local]))


def row_sum(block):
    return jnp.sum(jnp.transpose(block), axis=0, keepdims=True)


def weights_kernel(offs, acc_in, tiles, ext, gb, gg, *refs):
    halves, (acc, gw, gv, h2_hbm, sem) = (refs[:6], refs[6:12]), refs[12:]
    blk = tiles.shape[2]
    puts = [
        pltpu.make_async_copy(half[0], h2_hbm.at[pl.ds(rows_at(is_far), HALO)], sem.at[i])
        for i, (is_far, half) in enumerate(zip((True, False), halves))
    ]
    for c in puts:
        c.start()
    gv[0:1] = row_sum(gb[...])
    gv[1:2] = row_sum(gg[...])
    gw[...] = jnp.zeros_like(gw)
    for is_far, (_, agg, act, gmix, gpre, gagg) in zip((True, False), halves):
        base = rows_at(is_far)
        for_blocks(HALO, lambda b: push_inner(base + b, gagg[b], acc, HALO, tiles, offs, blk))

        def outer(it, c):
            local = [it * OUTER + s for s in range(OUTER)]
            outer_step(local, ext, HALO + base, agg, act, gmix, gpre, gw)
            return c

        lax.fori_loop(0, HALO // OUTER, outer, 0)
    for c in puts:
        c.wait()


def output_kernel(nb, h_hbm, out_hbm, h, out, sem):
    blk = h.shape[2]
    per = nb // sem.shape[0]

    def get(it):
        some = pl.ds(it * per, per)
        return pltpu.make_async_copy(h_hbm.at[some], h.at[some], sem.at[it])

    def put(it):
        rows = pl.ds(pl.multiple_of(it * per * blk, per * blk), per * blk)
        return pltpu.make_async_copy(out.at[rows], out_hbm.at[rows], sem.at[it])

    for it in range(nb // per):
        get(it).start()
    one = eye(blk)

    def step(it, c):
        get(it).wait()
        for s in range(per):
            b = it * per + s
            out[pl.ds(pl.multiple_of(b * blk, blk), blk)] = nt(one, h[b]).astype(BF16)
        put(it).start()
        return c

    lax.fori_loop(0, nb // per, step, 0)
    for it in range(nb // per):
        put(it).wait()


def node2_kernel(nb, is_far, offs, rim, acc_in, tiles, w_in, w2, gcols, kept, agg, act, slope, xhat, inv, *refs):
    if is_far:
        (gw1, gv1, *_, far_hbm, bundle_hbm, gagg_hbm, acc_hbm,
         acc, gb, gg, gw, gagg, gmix, gpre, rims, bundle, sem) = refs
    else:
        _, acc, gb, gg, gw, gagg_hbm, near_hbm, gagg, gmix, gpre, rims, sem = refs
        gb[...] = jnp.zeros_like(gb)
        gg[...] = jnp.zeros_like(gg)
        gw[...] = jnp.zeros_like(gw)
    blk = tiles.shape[2]
    gcol = gcols.at[0]
    base = rows_at(is_far)

    def unmix(it):
        local = chunk(0, it)
        grad = lanes([acc_in[HALO + base + b] + rim[b].astype(F32) for b in local])
        xhat_w = lanes([xhat[b] for b in local]).astype(F32)
        inv_w = lanes([inv[b] for b in local])
        prod, gmix_w, gact = unmix_step(grad, xhat_w, inv_w, w2[0], gcol)
        gg[...] += fold(prod, blk)
        for s, b in enumerate(local):
            gmix[b] = cut(gmix_w, s, blk)
        return gact, grad

    def unjoin(it, gact, grad):
        slope_w = lanes([slope[b] for b in chunk(0, it)]).astype(F32)
        gpre_f, gpre_w, gh, gagg_w = unjoin_step(gact, slope_w, w_in[0])
        gb[...] += fold(gpre_f, blk)
        return gpre_w, grad + gh, gagg_w

    def push(it, gpre_w, rest, gagg_w):
        for s, b in enumerate(chunk(0, it)):
            gpre[b] = cut(gpre_w, s, blk)
            gagg[b] = cut(gagg_w, s, blk)
            acc[HALO + base + b] += cut(rest, s, blk)
        some = pl.ds(it * CH, CH)
        pltpu.make_async_copy(gagg.at[some], gagg_hbm.at[some], sem.at[1]).start()
        push_edge(chunk(base, it), gagg_w, acc, tiles, offs, blk)
        if (it + 1) * CH % OUTER == 0:
            wide = list(range((it + 1) * CH - OUTER, (it + 1) * CH))
            outer_step(wide, kept, base, agg, act, gmix, gpre, gw)

    pipelined(HALO // CH, unmix, unjoin, push)
    at = rim_at(nb, is_far)

    def rim_sum(b):
        rims[b] = acc[at + b].astype(BF16)

    if is_far:
        put = pltpu.make_async_copy(acc.at[pl.ds(HALO, nb)], acc_hbm, sem.at[0])
        put.start()
    for_blocks(HALO, rim_sum, 8)
    sent = pltpu.make_async_copy(rims, far_hbm if is_far else near_hbm, sem.at[2])
    sent.start()
    if not is_far:
        pltpu.make_async_copy(gagg, gagg_hbm, sem.at[1]).wait()
        sent.wait()
        return
    devices = bundle.shape[0]
    rows = gw.shape[0]
    share = 2 * rows // devices
    vectors = jnp.concatenate([row_sum(gb[...]), row_sum(gg[...]), gv1[...]], axis=0)
    vectors = jnp.concatenate([vectors, jnp.zeros_like(vectors)], axis=0).astype(BF16)
    for p in range(devices):
        bundle[p, 0:8] = vectors
        first = p * share
        if first + share <= rows:
            mine = gw[first : first + share]
        elif first >= rows:
            mine = gw1[first - rows : first - rows + share]
        else:
            mine = jnp.concatenate([gw[first:rows], gw1[0 : first + share - rows]], axis=0)
        bundle[p, 8 : 8 + share] = mine.astype(BF16)
    out = pltpu.make_async_copy(bundle, bundle_hbm, sem.at[3])
    out.start()
    pltpu.make_async_copy(gagg, gagg_hbm, sem.at[1]).wait()
    for c in [sent, put, out]:
        c.wait()


def total_kernel(scale, parts, mine_hbm, gbias, ggain, mine, sem):
    total = jnp.sum(parts[...].astype(F32), axis=0) * scale
    mine[...] = jnp.broadcast_to(total[8:][None], mine.shape).astype(BF16)
    put = pltpu.make_async_copy(mine, mine_hbm, sem.at[0])
    put.start()
    gbias[0:1] = total[0:1]
    ggain[0:1] = total[1:2]
    gbias[1:2] = total[2:3]
    ggain[1:2] = total[3:4]
    put.wait()


def final_kernel(
    nb, offs, near, far, acc_hbm, gagg_far, gagg_near, tiles_hbm, out_hbm,
    acc, gagg, tiles, halo, out, sem, tsem,
):
    blk = tiles.shape[2]
    per = nb // tsem.shape[0]
    get_a = pltpu.make_async_copy(acc_hbm, acc, sem.at[0])

    def get_t(it):
        some = pl.ds(it * per, per)
        return pltpu.make_async_copy(tiles_hbm.at[some], tiles.at[some], tsem.at[it])

    get_g = fetch_rims(gagg_near, gagg_far, gagg, sem.at[pl.ds(4, 2)])
    get_a.start()
    for it in range(nb // per):
        get_t(it).start()
    rims = fetch_rims(near, far, halo, sem.at[pl.ds(2, 2)])
    for c in get_g:
        c.wait()
    get_a.wait()

    def push(it, c):
        get_t(it).wait()
        for s in range(per):
            push_inner(it * per + s, gagg[it * per + s], acc, 0, tiles, offs, blk)
        return c

    lax.fori_loop(0, nb // per, push, 0)

    for c in rims:
        c.wait()

    def put(it):
        rows = pl.ds(it * per * blk, per * blk)
        return pltpu.make_async_copy(out.at[rows], out_hbm.at[rows], tsem.at[it])

    def step(it, c):
        for s in range(per):
            b = it * per + s
            out[pl.ds(b * blk, blk)] = jnp.transpose(acc[b] + halo[b].astype(F32))
        put(it).start()
        return c

    lax.fori_loop(0, nb // per, step, 0)
    for it in range(nb // per):
        put(it).wait()


def unpack_kernel(sums, out1_hbm, out2_hbm, out1, out2, sem):
    devices, share, _ = sums.shape
    _, upper, _ = out1.shape
    rows = upper + out2.shape[1]
    for p in range(devices):
        mine = sums[p].astype(F32)
        at = p * share
        while at < (p + 1) * share:
            layer, row = divmod(at, rows)
            end = min((p + 1) * share, layer * rows + (upper if row < upper else rows))
            piece = mine[at - p * share : end - p * share]
            if row < upper:
                out1[layer, row : row + end - at] = piece
            else:
                out2[layer, row - upper : row - upper + end - at] = piece
            at = end
    puts = [
        pltpu.make_async_copy(out1, out1_hbm, sem.at[0]),
        pltpu.make_async_copy(out2, out2_hbm, sem.at[1]),
    ]
    for p in puts:
        p.start()
    for p in puts:
        p.wait()


def call(body, args, outs, scratch=(), alias=None, far_args=(), any_args=(), flops=0, moved=0):
    args = [
        pltpu.with_memory_space_constraint(a, pltpu.HBM) if i in far_args else a
        for i, a in enumerate(args)
    ]
    return pl.pallas_call(
        body,
        in_specs=[
            HBM if i in far_args else ANY if i in any_args else SMEM if a.dtype == jnp.int32 else VMEM
            for i, a in enumerate(args)
        ],
        out_specs=[HBM if len(o) == 3 else VMEM for o in outs],
        out_shape=[
            pltpu.HBM(o[0], o[1]) if len(o) == 3 else jax.ShapeDtypeStruct(o[0], o[1]) for o in outs
        ],
        scratch_shapes=list(scratch),
        input_output_aliases=alias or {},
        compiler_params=pltpu.CompilerParams(vmem_limit_bytes=24 << 20),
        cost_estimate=pl.CostEstimate(flops=flops, bytes_accessed=moved, transcendentals=0),
    )(*args)


def dma(n):
    return pltpu.SemaphoreType.DMA((n,))


def per_device(feats, tile_vals, tile_offs, w_in, bias_in, w_out, gain, cot):
    nodes, width = feats.shape
    nb, slots, blk, _ = tile_vals.shape
    hid = w_out.shape[1]
    layers = w_in.shape[0]
    assert nb == 2 * HALO and width == blk and hid == width and layers == 2
    devices = lax.axis_size("band") * lax.axis_size("rep")
    block = (width, blk)
    full, _, ext = ((n, *block) for n in (nb, HALO, nb + 2 * HALO))
    whole = (2 * width + hid, hid)
    share = layers * whole[0] // devices
    assert share * devices == layers * whole[0]
    v = pltpu.VMEM
    part_of = functools.partial
    tile_flops = 2 * blk * blk * width
    mlp_flops = 2 * nodes * (2 * width * hid + hid * width)
    mib = 2 * nodes * width
    offs = tile_offs.T

    half = (HALO, *block)
    half_rows = (nodes // 2, width)

    h0, far = call(
        turn_kernel, (feats,), [(ext, BF16), (half, BF16)],
        [v(half_rows, BF16), dma(4)], far_args=(0,),
        flops=nb * tile_flops, moved=3 * mib,
    )
    far = swap(far, True)
    h0, near, part, w1t, w2t, w2, bcols, gcols, kept = call(
        part_of(inner0_kernel, nb), (offs, h0, feats, tile_vals, w_in, w_out, bias_in, gain),
        [(ext, BF16), (half, BF16), (full, F32), ((layers, hid, 2 * width), BF16), ((layers, width, hid), BF16),
         (w_out.shape, BF16), ((layers, *block), F32), ((layers, *block), F32), (full, BF16, True)],
        [v(half_rows, BF16), v(tile_vals.shape, BF16), v(w_in.shape, BF16), v(w_out.shape, BF16), dma(4), dma(8)],
        {1: 0}, far_args=(2, 3, 4, 5),
        flops=2 * nb * tile_flops, moved=6 * mib,
    )
    near = swap(near, False)

    def node0(is_far, rim, h, more):
        return call(
            part_of(node0_kernel, nb, is_far),
            (offs, rim, h, part, tile_vals, w1t, w2t, bcols, gcols, *more),
            [(half, BF16), (ext, BF16), (ext, BF16), *[(half, BF16)] * 4, ((HALO, 1, blk), F32)],
            alias={2: 1} if is_far else {2: 1, 9: 2},
            flops=(nb * tile_flops + mlp_flops) // 2, moved=6 * mib,
        )

    far, h0, h1, *saved_far = node0(True, far, h0, ())
    far = swap(far, True)
    near, h0, h1, *saved_near = node0(False, near, h0, (h1,))
    near = swap(near, False)
    part, cott, acc1, acc0 = call(
        part_of(inner1_kernel, nb), (offs, h1, tile_vals, cot), [(full, F32), (full, BF16), (ext, F32), (ext, F32)],
        flops=2 * nb * tile_flops, moved=8 * mib,
    )

    def node1(is_far, rim, h, more):
        return call(
            part_of(node1_kernel, nb, is_far),
            (offs, rim, h, part, tile_vals, cott, w1t, w2t, w_in, w2, bcols, gcols, *more),
            [(half, BF16), (ext, BF16), *[(half, BF16)] * 6, (ext, F32), (block, F32), (block, F32)],
            alias={2: 1, 12: 8} if is_far else {2: 1, 12: 8, 13: 9, 14: 10},
            flops=nb * tile_flops + mlp_flops, moved=8 * mib,
        )

    far, h1, *made_far, acc, gb1, gg1 = node1(True, far, h1, (acc1,))
    far = swap(far, True)
    near, h1, *made_near, acc, gb1, gg1 = node1(False, near, h1, (acc, gb1, gg1))
    near = swap(near, False)
    acc, gw1, gv1, h2 = call(
        weights_kernel, (offs, acc, tile_vals, h1, gb1, gg1, *made_far, *made_near),
        [(ext, F32), (whole, F32), ((2, hid), F32), (full, BF16, True)],
        [dma(2)], {1: 0},
        flops=tile_flops, moved=mib,
    )

    def node2(is_far, rim, acc, saved, more, outs, scratch, alias):
        return call(
            part_of(node2_kernel, nb, is_far),
            (offs, rim, acc, tile_vals, w_in, w2, gcols, kept, *saved, *more), outs, scratch, alias,
            flops=nb * tile_flops + mlp_flops, moved=8 * mib,
        )

    sums = [(ext, F32), (block, F32), (block, F32), (whole, F32)]
    work = [v(half, BF16)] * 4
    *state, gagg_near, near = node2(
        False, near, acc, saved_near, (acc0,), [*sums, (half, BF16, True), (half, BF16, True)], [*work, dma(3)], {13: 0}
    )
    far, bundle, gagg_far, acc, *_ = node2(
        True, far, acc, saved_far, (gw1, gv1, *state),
        [(half, BF16, True), ((devices, 8 + share, hid), BF16, True), (half, BF16, True), (full, F32, True), *sums],
        [*work, v((devices, 8 + share, hid), BF16), dma(4)],
        {15 + i: 4 + i for i in range(4)},
    )

    parts = lax.all_to_all(bundle, AXES, 0, 0, tiled=True)
    near, far = swap(near, False), swap(far, True)
    (out_feats,) = call(
        part_of(output_kernel, nb), (h2,), [((nodes, width), BF16, True)],
        [v(full, BF16), v((nodes, width), BF16), dma(4)], far_args=(0,),
        flops=nb * tile_flops, moved=2 * mib,
    )
    mine, grad_bias, grad_gain = call(
        part_of(total_kernel, 1.0 / math.sqrt(nodes * devices)), (parts,),
        [((devices, share, hid), BF16, True), ((layers, hid), F32), ((layers, width), F32)],
        [v((devices, share, hid), BF16), dma(1)],
        flops=nodes * width, moved=mib,
    )
    sums = lax.all_to_all(mine, AXES, 0, 0, tiled=True)
    (grad_feats,) = call(
        part_of(final_kernel, nb), (offs, near, far, acc, gagg_far, gagg_near, tile_vals),
        [((nodes, width), F32, True)],
        [v(full, F32), v(full, BF16), v((nb, slots, blk, blk), BF16), v(full, BF16), v((nodes, width), F32), dma(6), dma(8)],
        far_args=(3, 4, 5, 6), any_args=(1, 2),
        flops=2 * nb * tile_flops, moved=9 * mib,
    )
    grad_w_in, grad_w_out = call(
        unpack_kernel, (sums,),
        [((layers, 2 * width, hid), F32, True), ((layers, hid, width), F32, True)],
        [v((layers, 2 * width, hid), F32), v((layers, hid, width), F32), dma(2)],
        flops=nodes * width, moved=mib,
    )
    return out_feats, grad_feats, grad_w_in, grad_bias, grad_w_out, grad_gain


def solution(mesh):
    placed = (
        P(AXES, None),
        P(AXES, None, None, None),
        P(AXES, None),
        P(),
        P(),
        P(),
        P(),
        P(AXES, None),
    )
    return jax.shard_map(
        per_device,
        mesh=mesh,
        in_specs=placed,
        out_specs=(P(AXES, None), P(AXES, None), P(), P(), P(), P()),
        check_vma=False,
    )
```

```python
import functools
import math

import jax
import jax.numpy as jnp
from jax import lax
from jax.experimental import pallas as pl
from jax.experimental.pallas import tpu as pltpu
from jax.sharding import PartitionSpec as P


HALO = 16
EPS = 1e-05
AXES = ("band", "rep")
F32 = jnp.float32
BF16 = jnp.bfloat16
OUTER = 8
CH = 4
HBM = pl.BlockSpec(memory_space=pltpu.HBM)
ANY = pl.BlockSpec(memory_space=pl.ANY)
SMEM = pl.BlockSpec(memory_space=pltpu.SMEM)
VMEM = pl.BlockSpec(memory_space=pltpu.VMEM)


def nt(a, b):
    return lax.dot_general(a, b, (((1,), (1,)), ((), ())), preferred_element_type=F32)


def nn(a, b):
    return jnp.dot(a, b, preferred_element_type=F32)


def eye(n):
    rows = lax.broadcasted_iota(jnp.int32, (n, n), 0)
    cols = lax.broadcasted_iota(jnp.int32, (n, n), 1)
    return (rows == cols).astype(BF16)


def column(row, width):
    return jnp.transpose(jnp.broadcast_to(row, (width, row.shape[1])))


def lanes(parts):
    return jnp.concatenate(parts, axis=1)


def widen(block, times):
    return lanes([block] * times)


def parity():
    place = lax.axis_index("band") * lax.axis_size("rep") + lax.axis_index("rep")
    return lax.rem(place, 2)


def swap(x, far):
    n = lax.axis_size("band") * lax.axis_size("rep")
    pairs = []
    for c in range(n // 2):
        a, b = (2 * c, 2 * c + 1) if not far else (2 * c + 1, (2 * c + 2) % n)
        pairs += [(a, b), (b, a)]
    return lax.ppermute(x, AXES, pairs)


def rim_at(nb, far):
    odd = parity()
    return (odd if far else 1 - odd) * (HALO + nb)


def quarter(nb, nearest):
    odd = parity()
    q = HALO // 2
    if nearest:
        return odd * (HALO + q), odd * q, q + odd * (nb + q)
    return q + odd * (HALO - q), q - odd * q, odd * (nb + HALO + q)


def rows_at(far):
    odd = parity()
    return (odd if far else 1 - odd) * HALO


def pipelined(count, *stages):
    held = {}
    for t in range(count + len(stages) - 1):
        for i, stage in enumerate(stages):
            if 0 <= t - i < count:
                held[t - i] = stage(t - i, *held.get(t - i, ()))


def for_blocks(count, body, per=4):
    def step(it, c):
        for s in range(per):
            body(it * per + s)
        return c

    lax.fori_loop(0, count // per, step, 0)


def turn_rows(x, ext, out, base, one):
    blk = ext.shape[2]

    def turn(b):
        block = nt(one, x[pl.ds(b * blk, blk)]).astype(BF16)
        ext[HALO + base + b] = block
        out[b] = block

    for_blocks(HALO, turn, 8)


def half_of(x_hbm, x, base, sem):
    rows = x.shape[0]
    return pltpu.make_async_copy(
        x_hbm.at[pl.ds(pl.multiple_of(base * (rows // HALO), rows), rows)], x, sem
    )


def turn_kernel(nb, x_hbm, ext, near_border, outer, x, sem):
    blk = ext.shape[2]
    q = HALO // 2
    starts = [quarter(nb, True)[0], quarter(nb, False)[0]]
    pieces = sem.shape[0]
    per = HALO // pieces

    def get(i):
        rows = per * blk
        first = starts[i * per // q] + i * per % q
        return pltpu.make_async_copy(
            x_hbm.at[pl.ds(pl.multiple_of(first * blk, rows), rows)],
            x.at[pl.ds(i * rows, rows)],
            sem.at[i],
        )

    for i in range(pieces):
        get(i).start()
    one = eye(blk)
    for i in range(pieces):
        get(i).wait()
        for b in range(i * per, (i + 1) * per):
            block = nt(one, x[b * blk : (b + 1) * blk]).astype(BF16)
            ext[HALO + starts[b // q] + b % q] = block
            if b < q:
                near_border[b] = block
            else:
                outer[b - q] = block


def fetch_rims(near_hbm, far_hbm, rims, sem):
    copies = [
        pltpu.make_async_copy(far_hbm, rims.at[pl.ds(rows_at(True), HALO)], sem.at[0]),
        pltpu.make_async_copy(near_hbm, rims.at[pl.ds(rows_at(False), HALO)], sem.at[1]),
    ]
    for c in copies:
        c.start()
    return copies


def take_rim(rim, buf, at):
    def one(b):
        buf[at + b] = rim[b]

    for_blocks(rim.shape[0], one, 8)


def inner_tile(b, ext, tiles, offs, part):
    slot = jnp.where(b < HALO, 2, 1)
    left = lanes([ext[HALO + b], ext[HALO + b + offs[slot, b]]])
    part[b] = nt(left, lanes([tiles[b, 0], tiles[b, slot]]))


def inner0_kernel(
    nb, offs, ext_in, x_hbm, tiles_hbm, w_in_hbm, w_out_hbm, bias, gain,
    ext, near, part, w1t, w2t, w2, bcols, gcols, kept, x, tiles, w_in, w_out, sem, tsem,
):
    base = rows_at(False)
    per = nb // tsem.shape[0]

    def get_t(it):
        some = pl.ds(it * per, per)
        return pltpu.make_async_copy(tiles_hbm.at[some], tiles.at[some], tsem.at[it])

    get = half_of(x_hbm, x, base, sem.at[1])
    gets = [
        pltpu.make_async_copy(w_in_hbm, w_in, sem.at[2]),
        pltpu.make_async_copy(w_out_hbm, w_out, sem.at[3]),
    ]
    get.start()
    for it in range(nb // per):
        get_t(it).start()
    for c in gets:
        c.start()
    one = eye(tiles.shape[2])
    get.wait()
    turn_rows(x, ext, near, base, one)
    keep = pltpu.make_async_copy(ext.at[pl.ds(HALO, nb)], kept, sem.at[0])
    keep.start()

    def step(it, c):
        get_t(it).wait()
        for s in range(per):
            inner_tile(it * per + s, ext, tiles, offs, part)
        return c

    lax.fori_loop(0, nb // per, step, 0)
    for c in gets:
        c.wait()
    for layer in range(w_in.shape[0]):
        w1t[layer] = (0.5 * nt(one, w_in[layer])).astype(BF16)
        w2t[layer] = nt(one, w_out[layer]).astype(BF16)
        w2[layer] = (0.5 * w_out[layer].astype(F32)).astype(BF16)
        bcols[layer] = column(0.5 * bias[layer : layer + 1], bcols.shape[2])
        gcols[layer] = column(gain[layer : layer + 1], gcols.shape[2])
    keep.wait()


def inner1_kernel(nb, offs, ext, tiles, cot, part, cott, acc1, acc0):
    for_blocks(nb, lambda b: inner_tile(b, ext, tiles, offs, part))
    blk = tiles.shape[2]
    one = eye(blk)

    def turn(b):
        cott[b] = nt(one, cot[pl.ds(b * blk, blk)]).astype(BF16)

    for_blocks(nb, turn)
    clear(acc1)
    clear(acc0)


def edge_slot(b):
    return jnp.where(b < HALO, 1, 2)


def join_step(blocks, ext, part, tiles, offs, w1t, bias):
    agg = []
    for b in blocks:
        slot = edge_slot(b)
        agg.append((part[b] + nt(ext[HALO + b + offs[slot, b]], tiles[b, slot])).astype(BF16))
    agg = lanes(agg)
    feats = lanes([ext[HALO + b] for b in blocks])
    half = nn(w1t, jnp.concatenate([feats, agg], axis=0)) + widen(bias[...], CH)
    return feats, agg, half


def mix_step(half, w2t):
    t = jnp.tanh(half)
    up = 1.0 + t
    act = (half * up).astype(BF16)
    slope = up * (1.0 + half * (1.0 - t))
    return act, slope, nn(w2t, act)


def norm_step(feats, mix, gain):
    centred = mix - jnp.mean(mix, axis=0, keepdims=True)
    inv = lax.rsqrt(jnp.mean(centred * centred, axis=0, keepdims=True) + EPS)
    xhat = centred * inv
    after = (feats.astype(F32) + xhat * widen(gain[...], CH)).astype(BF16)
    return xhat, inv, after


def unmix_step(grad, xhat, inv, w2, gain):
    wide = widen(gain[...], CH)
    prod = grad * xhat
    gx = grad * wide
    gmix = inv * (
        gx - jnp.mean(gx, axis=0, keepdims=True) - xhat * jnp.mean(prod * wide, axis=0, keepdims=True)
    )
    gmix = gmix.astype(BF16)
    return prod, gmix, nn(w2, gmix)


def unjoin_step(gact, slope, w1):
    gpre = gact * slope
    gpre_b = gpre.astype(BF16)
    gcat = nn(w1, gpre_b)
    width = gact.shape[0]
    return gpre, gpre_b, gcat[:width], gcat[width:].astype(BF16)


def chunk(base, it):
    return [base + it * CH + s for s in range(CH)]


def cut(wide, s, blk):
    return wide[:, s * blk : (s + 1) * blk]


def fold(wide, blk):
    total = cut(wide, 0, blk)
    for s in range(1, CH):
        total = total + cut(wide, s, blk)
    return total


def push_edge(blocks, gagg, acc, tiles, offs, blk):
    for s, b in enumerate(blocks):
        slot = edge_slot(b)
        acc[HALO + b + offs[slot, b]] += nn(cut(gagg, s, blk), tiles[b, slot])


def push_inner(b, gagg, acc, first, tiles, offs, blk):
    slot = jnp.where(b < HALO, 2, 1)
    both = nn(gagg, lanes([tiles[b, 0], tiles[b, slot]]))
    acc[first + b] += both[:, :blk]
    acc[first + b + offs[slot, b]] += both[:, blk:]


def clear(ref):
    def one(b):
        ref[b] = jnp.zeros(ref.shape[1:], ref.dtype)

    for_blocks(ref.shape[0], one)


def node0_kernel(
    nb, kind, offs, rim, ext_in, part, tiles, w1t, w2t, bcols, gcols, *refs
):
    rim_out, ext, after_ext, agg, act, slope, xhat, inv = refs[{"outer": 0, "nearest": 6, "near": 1}[kind] :]
    bcol, gcol = bcols.at[0], gcols.at[0]
    blk = tiles.shape[2]
    if kind == "near":
        base, local, at = rows_at(False), 0, rim_at(nb, False)
    else:
        base, local, _ = quarter(nb, kind == "nearest")
        at = quarter(nb, kind == "outer")[2]
    take_rim(rim, ext, at)

    def join(it):
        return join_step(chunk(base, it), ext, part, tiles, offs, w1t[0], bcol)

    def mixing(it, feats, agg_w, half):
        for s, b in enumerate(chunk(local, it)):
            agg[b] = cut(agg_w, s, blk)
        return feats, *mix_step(half, w2t[0])

    def norm(it, feats, act_w, slope_w, mix):
        xhat_w, inv_w, after = norm_step(feats, mix, gcol)
        slope_w, xhat_w = slope_w.astype(BF16), xhat_w.astype(BF16)
        for s, b in enumerate(chunk(local, it)):
            act[b] = cut(act_w, s, blk)
            slope[b] = cut(slope_w, s, blk)
            xhat[b] = cut(xhat_w, s, blk)
            inv[b] = cut(inv_w, s, blk)
            after_ext[HALO + base + it * CH + s] = cut(after, s, blk)
            rim_out[it * CH + s] = cut(after, s, blk)

    pipelined(rim_out.shape[0] // CH, join, mixing, norm)


def node1_kernel(
    nb, is_far, offs, rim, ext_in, part, tiles, cott, w1t, w2t, w_in, w2, bcols, gcols, *refs
):
    rim_out, ext, h2, agg, act, gmix, gpre, gagg, acc, gb, gg = refs[2:] if is_far else refs[3:]
    bcol, gcol = bcols.at[1], gcols.at[1]
    blk = tiles.shape[2]
    if is_far:
        gb[...] = jnp.zeros_like(gb)
        gg[...] = jnp.zeros_like(gg)
    if is_far:
        take_rim(rim, ext, quarter(nb, True)[2])
        take_rim(refs[1], ext, quarter(nb, False)[2])
    else:
        take_rim(rim, ext, rim_at(nb, False))
    base = rows_at(is_far)

    def join(it):
        return join_step(chunk(base, it), ext, part, tiles, offs, w1t[1], bcol)

    def mixing(it, feats, agg_w, half):
        for s, b in enumerate(chunk(0, it)):
            agg[b] = cut(agg_w, s, blk)
        return feats, *mix_step(half, w2t[1])

    def turn(it, feats, act_w, slope, mix):
        xhat, inv, after = norm_step(feats, mix, gcol)
        grad = lanes([cott[b] for b in chunk(base, it)]).astype(F32)
        prod, gmix_w, gact = unmix_step(grad, xhat, inv, w2[1], gcol)
        gg[...] += fold(prod, blk)
        for s, b in enumerate(chunk(0, it)):
            act[b] = cut(act_w, s, blk)
            h2[b] = cut(after, s, blk)
            gmix[b] = cut(gmix_w, s, blk)
        return slope, gact

    def unjoin(it, slope, gact):
        gpre_f, gpre_w, gh, gagg_w = unjoin_step(gact, slope, w_in[1])
        gb[...] += fold(gpre_f, blk)
        grad = lanes([cott[b] for b in chunk(base, it)]).astype(F32)
        return gpre_w, grad + gh, gagg_w

    def push(it, gpre_w, rest, gagg_w):
        for s, b in enumerate(chunk(0, it)):
            gpre[b] = cut(gpre_w, s, blk)
            gagg[b] = cut(gagg_w, s, blk)
            acc[HALO + base + b] += cut(rest, s, blk)
        push_edge(chunk(base, it), gagg_w, acc, tiles, offs, blk)

    pipelined(HALO // CH, join, mixing, turn, unjoin, push)
    at = rim_at(nb, is_far)

    def give(b):
        rim_out[b] = acc[at + b].astype(BF16)

    for_blocks(HALO, give, 8)


def outer_step(local, feats, first, agg, act, gmix, gpre, gw):
    width = feats.shape[1]
    gpre_w = lanes([gpre[b] for b in local])
    gw[0:width] += nt(lanes([feats[first + b] for b in local]), gpre_w)
    gw[width : 2 * width] += nt(lanes([agg[b] for b in local]), gpre_w)
    gw[2 * width :] += nt(lanes([act[b] for b in local]), lanes([gmix[b] for b in local]))


def row_sum(block):
    return jnp.sum(jnp.transpose(block), axis=0, keepdims=True)


def weights_kernel(offs, acc_in, tiles, ext, gb, gg, *refs):
    halves, (acc, gw, gv, h2_hbm, sem) = (refs[:6], refs[6:12]), refs[12:]
    blk = tiles.shape[2]
    puts = [
        pltpu.make_async_copy(half[0], h2_hbm.at[pl.ds(rows_at(is_far), HALO)], sem.at[i])
        for i, (is_far, half) in enumerate(zip((True, False), halves))
    ]
    for c in puts:
        c.start()
    gv[0:1] = row_sum(gb[...])
    gv[1:2] = row_sum(gg[...])
    gw[...] = jnp.zeros_like(gw)
    for is_far, (_, agg, act, gmix, gpre, gagg) in zip((True, False), halves):
        base = rows_at(is_far)
        for_blocks(HALO, lambda b: push_inner(base + b, gagg[b], acc, HALO, tiles, offs, blk))

        def outer(it, c):
            local = [it * OUTER + s for s in range(OUTER)]
            outer_step(local, ext, HALO + base, agg, act, gmix, gpre, gw)
            return c

        lax.fori_loop(0, HALO // OUTER, outer, 0)
    for c in puts:
        c.wait()


def output_kernel(nb, h_hbm, out_hbm, h, out, sem):
    blk = h.shape[2]
    per = nb // sem.shape[0]

    def get(it):
        some = pl.ds(it * per, per)
        return pltpu.make_async_copy(h_hbm.at[some], h.at[some], sem.at[it])

    def put(it):
        rows = pl.ds(pl.multiple_of(it * per * blk, per * blk), per * blk)
        return pltpu.make_async_copy(out.at[rows], out_hbm.at[rows], sem.at[it])

    for it in range(nb // per):
        get(it).start()
    one = eye(blk)

    def step(it, c):
        get(it).wait()
        for s in range(per):
            b = it * per + s
            out[pl.ds(pl.multiple_of(b * blk, blk), blk)] = nt(one, h[b]).astype(BF16)
        put(it).start()
        return c

    lax.fori_loop(0, nb // per, step, 0)
    for it in range(nb // per):
        put(it).wait()


def node2_kernel(nb, is_far, offs, rim, acc_in, tiles, w_in, w2, gcols, kept, agg, act, slope, xhat, inv, *refs):
    if is_far:
        (gw1, gv1, *_, far_hbm, bundle_hbm, gagg_hbm, acc_hbm,
         acc, gb, gg, gw, gagg, gmix, gpre, rims, bundle, sem) = refs
    else:
        _, acc, gb, gg, gw, gagg_hbm, near_hbm, gagg, gmix, gpre, rims, sem = refs
        gb[...] = jnp.zeros_like(gb)
        gg[...] = jnp.zeros_like(gg)
        gw[...] = jnp.zeros_like(gw)
    blk = tiles.shape[2]
    gcol = gcols.at[0]
    base = rows_at(is_far)

    def unmix(it):
        local = chunk(0, it)
        grad = lanes([acc_in[HALO + base + b] + rim[b].astype(F32) for b in local])
        xhat_w = lanes([xhat[b] for b in local]).astype(F32)
        inv_w = lanes([inv[b] for b in local])
        prod, gmix_w, gact = unmix_step(grad, xhat_w, inv_w, w2[0], gcol)
        gg[...] += fold(prod, blk)
        for s, b in enumerate(local):
            gmix[b] = cut(gmix_w, s, blk)
        return gact, grad

    def unjoin(it, gact, grad):
        slope_w = lanes([slope[b] for b in chunk(0, it)]).astype(F32)
        gpre_f, gpre_w, gh, gagg_w = unjoin_step(gact, slope_w, w_in[0])
        gb[...] += fold(gpre_f, blk)
        return gpre_w, grad + gh, gagg_w

    def push(it, gpre_w, rest, gagg_w):
        for s, b in enumerate(chunk(0, it)):
            gpre[b] = cut(gpre_w, s, blk)
            gagg[b] = cut(gagg_w, s, blk)
            acc[HALO + base + b] += cut(rest, s, blk)
        some = pl.ds(it * CH, CH)
        pltpu.make_async_copy(gagg.at[some], gagg_hbm.at[some], sem.at[1]).start()
        push_edge(chunk(base, it), gagg_w, acc, tiles, offs, blk)
        if (it + 1) * CH % OUTER == 0:
            wide = list(range((it + 1) * CH - OUTER, (it + 1) * CH))
            outer_step(wide, kept, base, agg, act, gmix, gpre, gw)

    pipelined(HALO // CH, unmix, unjoin, push)
    at = rim_at(nb, is_far)

    def rim_sum(b):
        rims[b] = acc[at + b].astype(BF16)

    if is_far:
        put = pltpu.make_async_copy(acc.at[pl.ds(HALO, nb)], acc_hbm, sem.at[0])
        put.start()
    for_blocks(HALO, rim_sum, 8)
    sent = pltpu.make_async_copy(rims, far_hbm if is_far else near_hbm, sem.at[2])
    sent.start()
    if not is_far:
        pltpu.make_async_copy(gagg, gagg_hbm, sem.at[1]).wait()
        sent.wait()
        return
    devices = bundle.shape[0]
    rows = gw.shape[0]
    share = 2 * rows // devices
    vectors = jnp.concatenate([row_sum(gb[...]), row_sum(gg[...]), gv1[...]], axis=0)
    vectors = jnp.concatenate([vectors, jnp.zeros_like(vectors)], axis=0).astype(BF16)
    for p in range(devices):
        bundle[p, 0:8] = vectors
        first = p * share
        if first + share <= rows:
            mine = gw[first : first + share]
        elif first >= rows:
            mine = gw1[first - rows : first - rows + share]
        else:
            mine = jnp.concatenate([gw[first:rows], gw1[0 : first + share - rows]], axis=0)
        bundle[p, 8 : 8 + share] = mine.astype(BF16)
    out = pltpu.make_async_copy(bundle, bundle_hbm, sem.at[3])
    out.start()
    pltpu.make_async_copy(gagg, gagg_hbm, sem.at[1]).wait()
    for c in [sent, put, out]:
        c.wait()


def total_kernel(scale, parts, mine_hbm, gbias, ggain, mine, sem):
    total = jnp.sum(parts[...].astype(F32), axis=0) * scale
    mine[...] = jnp.broadcast_to(total[8:][None], mine.shape).astype(BF16)
    put = pltpu.make_async_copy(mine, mine_hbm, sem.at[0])
    put.start()
    gbias[0:1] = total[0:1]
    ggain[0:1] = total[1:2]
    gbias[1:2] = total[2:3]
    ggain[1:2] = total[3:4]
    put.wait()


def final_kernel(
    nb, offs, near, far, acc_hbm, gagg_far, gagg_near, tiles_hbm, out_hbm,
    acc, gagg, tiles, halo, out, sem, tsem,
):
    blk = tiles.shape[2]
    per = nb // tsem.shape[0]
    get_a = pltpu.make_async_copy(acc_hbm, acc, sem.at[0])

    def get_t(it):
        some = pl.ds(it * per, per)
        return pltpu.make_async_copy(tiles_hbm.at[some], tiles.at[some], tsem.at[it])

    get_g = fetch_rims(gagg_near, gagg_far, gagg, sem.at[pl.ds(4, 2)])
    get_a.start()
    for it in range(nb // per):
        get_t(it).start()
    rims = fetch_rims(near, far, halo, sem.at[pl.ds(2, 2)])
    for c in get_g:
        c.wait()
    get_a.wait()

    def push(it, c):
        get_t(it).wait()
        for s in range(per):
            push_inner(it * per + s, gagg[it * per + s], acc, 0, tiles, offs, blk)
        return c

    lax.fori_loop(0, nb // per, push, 0)

    for c in rims:
        c.wait()

    def put(it):
        rows = pl.ds(it * per * blk, per * blk)
        return pltpu.make_async_copy(out.at[rows], out_hbm.at[rows], tsem.at[it])

    def step(it, c):
        for s in range(per):
            b = it * per + s
            out[pl.ds(b * blk, blk)] = jnp.transpose(acc[b] + halo[b].astype(F32))
        put(it).start()
        return c

    lax.fori_loop(0, nb // per, step, 0)
    for it in range(nb // per):
        put(it).wait()


def unpack_kernel(sums, out1_hbm, out2_hbm, out1, out2, sem):
    devices, share, _ = sums.shape
    _, upper, _ = out1.shape
    rows = upper + out2.shape[1]
    for p in range(devices):
        mine = sums[p].astype(F32)
        at = p * share
        while at < (p + 1) * share:
            layer, row = divmod(at, rows)
            end = min((p + 1) * share, layer * rows + (upper if row < upper else rows))
            piece = mine[at - p * share : end - p * share]
            if row < upper:
                out1[layer, row : row + end - at] = piece
            else:
                out2[layer, row - upper : row - upper + end - at] = piece
            at = end
    puts = [
        pltpu.make_async_copy(out1, out1_hbm, sem.at[0]),
        pltpu.make_async_copy(out2, out2_hbm, sem.at[1]),
    ]
    for p in puts:
        p.start()
    for p in puts:
        p.wait()


def call(body, args, outs, scratch=(), alias=None, far_args=(), any_args=(), flops=0, moved=0):
    args = [
        pltpu.with_memory_space_constraint(a, pltpu.HBM) if i in far_args else a
        for i, a in enumerate(args)
    ]
    return pl.pallas_call(
        body,
        in_specs=[
            HBM if i in far_args else ANY if i in any_args else SMEM if a.dtype == jnp.int32 else VMEM
            for i, a in enumerate(args)
        ],
        out_specs=[HBM if len(o) == 3 else VMEM for o in outs],
        out_shape=[
            pltpu.HBM(o[0], o[1]) if len(o) == 3 else jax.ShapeDtypeStruct(o[0], o[1]) for o in outs
        ],
        scratch_shapes=list(scratch),
        input_output_aliases=alias or {},
        compiler_params=pltpu.CompilerParams(vmem_limit_bytes=24 << 20),
        cost_estimate=pl.CostEstimate(flops=flops, bytes_accessed=moved, transcendentals=0),
    )(*args)


def dma(n):
    return pltpu.SemaphoreType.DMA((n,))


def per_device(feats, tile_vals, tile_offs, w_in, bias_in, w_out, gain, cot):
    nodes, width = feats.shape
    nb, slots, blk, _ = tile_vals.shape
    hid = w_out.shape[1]
    layers = w_in.shape[0]
    assert nb == 2 * HALO and width == blk and hid == width and layers == 2
    devices = lax.axis_size("band") * lax.axis_size("rep")
    block = (width, blk)
    full, _, ext = ((n, *block) for n in (nb, HALO, nb + 2 * HALO))
    whole = (2 * width + hid, hid)
    share = layers * whole[0] // devices
    assert share * devices == layers * whole[0]
    v = pltpu.VMEM
    part_of = functools.partial
    tile_flops = 2 * blk * blk * width
    mlp_flops = 2 * nodes * (2 * width * hid + hid * width)
    mib = 2 * nodes * width
    offs = tile_offs.T

    half = (HALO, *block)
    half_rows = (nodes // 2, width)

    some = (HALO // 2, *block)
    h0, border, outer = call(
        part_of(turn_kernel, nb), (feats,), [(ext, BF16), (some, BF16), (some, BF16)],
        [v(half_rows, BF16), dma(4)], far_args=(0,),
        flops=nb * tile_flops, moved=3 * mib,
    )
    border = swap(border, True)
    outer = swap(outer, True)
    h0, near, part, w1t, w2t, w2, bcols, gcols, kept = call(
        part_of(inner0_kernel, nb), (offs, h0, feats, tile_vals, w_in, w_out, bias_in, gain),
        [(ext, BF16), (half, BF16), (full, F32), ((layers, hid, 2 * width), BF16), ((layers, width, hid), BF16),
         (w_out.shape, BF16), ((layers, *block), F32), ((layers, *block), F32), (full, BF16, True)],
        [v(half_rows, BF16), v(tile_vals.shape, BF16), v(w_in.shape, BF16), v(w_out.shape, BF16), dma(4), dma(8)],
        {1: 0}, far_args=(2, 3, 4, 5),
        flops=2 * nb * tile_flops, moved=6 * mib,
    )
    near = swap(near, False)

    def node0(kind, rim, h, more):
        alias = {2: 1} | {9 + i: 2 + i for i in range(len(more))}
        return call(
            part_of(node0_kernel, nb, kind),
            (offs, rim, h, part, tile_vals, w1t, w2t, bcols, gcols, *more),
            [(rim.shape, BF16), (ext, BF16), (ext, BF16), *[(half, BF16)] * 4, ((HALO, 1, blk), F32)],
            alias=alias,
            flops=(nb * tile_flops + mlp_flops) // 4, moved=4 * mib,
        )

    next_outer, h0, *saved_far = node0("outer", border, h0, ())
    next_outer = swap(next_outer, True)
    border, h0, *saved_far = node0("nearest", outer, h0, saved_far)
    border = swap(border, True)
    near, h0, h1, *saved_near = node0("near", near, h0, saved_far[:1])
    saved_far = saved_far[1:]
    near = swap(near, False)
    part, cott, acc1, acc0 = call(
        part_of(inner1_kernel, nb), (offs, h1, tile_vals, cot), [(full, F32), (full, BF16), (ext, F32), (ext, F32)],
        flops=2 * nb * tile_flops, moved=8 * mib,
    )

    def node1(is_far, rim, h, more):
        return call(
            part_of(node1_kernel, nb, is_far),
            (offs, rim, h, part, tile_vals, cott, w1t, w2t, w_in, w2, bcols, gcols, *more),
            [(half, BF16), (ext, BF16), *[(half, BF16)] * 6, (ext, F32), (block, F32), (block, F32)],
            alias={2: 1, 12: 8} if is_far else {2: 1, 12: 8, 13: 9, 14: 10},
            flops=nb * tile_flops + mlp_flops, moved=8 * mib,
        )

    far, h1, *made_far, acc, gb1, gg1 = node1(True, border, h1, (acc1, next_outer))
    far = swap(far, True)
    near, h1, *made_near, acc, gb1, gg1 = node1(False, near, h1, (acc, gb1, gg1))
    near = swap(near, False)
    acc, gw1, gv1, h2 = call(
        weights_kernel, (offs, acc, tile_vals, h1, gb1, gg1, *made_far, *made_near),
        [(ext, F32), (whole, F32), ((2, hid), F32), (full, BF16, True)],
        [dma(2)], {1: 0},
        flops=tile_flops, moved=mib,
    )

    def node2(is_far, rim, acc, saved, more, outs, scratch, alias):
        return call(
            part_of(node2_kernel, nb, is_far),
            (offs, rim, acc, tile_vals, w_in, w2, gcols, kept, *saved, *more), outs, scratch, alias,
            flops=nb * tile_flops + mlp_flops, moved=8 * mib,
        )

    sums = [(ext, F32), (block, F32), (block, F32), (whole, F32)]
    work = [v(half, BF16)] * 4
    *state, gagg_near, near = node2(
        False, near, acc, saved_near, (acc0,), [*sums, (half, BF16, True), (half, BF16, True)], [*work, dma(3)], {13: 0}
    )
    far, bundle, gagg_far, acc, *_ = node2(
        True, far, acc, saved_far, (gw1, gv1, *state),
        [(half, BF16, True), ((devices, 8 + share, hid), BF16, True), (half, BF16, True), (full, F32, True), *sums],
        [*work, v((devices, 8 + share, hid), BF16), dma(4)],
        {15 + i: 4 + i for i in range(4)},
    )

    parts = lax.all_to_all(bundle, AXES, 0, 0, tiled=True)
    near, far = swap(near, False), swap(far, True)
    (out_feats,) = call(
        part_of(output_kernel, nb), (h2,), [((nodes, width), BF16, True)],
        [v(full, BF16), v((nodes, width), BF16), dma(4)], far_args=(0,),
        flops=nb * tile_flops, moved=2 * mib,
    )
    mine, grad_bias, grad_gain = call(
        part_of(total_kernel, 1.0 / math.sqrt(nodes * devices)), (parts,),
        [((devices, share, hid), BF16, True), ((layers, hid), F32), ((layers, width), F32)],
        [v((devices, share, hid), BF16), dma(1)],
        flops=nodes * width, moved=mib,
    )
    sums = lax.all_to_all(mine, AXES, 0, 0, tiled=True)
    (grad_feats,) = call(
        part_of(final_kernel, nb), (offs, near, far, acc, gagg_far, gagg_near, tile_vals),
        [((nodes, width), F32, True)],
        [v(full, F32), v(full, BF16), v((nb, slots, blk, blk), BF16), v(full, BF16), v((nodes, width), F32), dma(6), dma(8)],
        far_args=(3, 4, 5, 6), any_args=(1, 2),
        flops=2 * nb * tile_flops, moved=9 * mib,
    )
    grad_w_in, grad_w_out = call(
        unpack_kernel, (sums,),
        [((layers, 2 * width, hid), F32, True), ((layers, hid, width), F32, True)],
        [v((layers, 2 * width, hid), F32), v((layers, hid, width), F32), dma(2)],
        flops=nodes * width, moved=mib,
    )
    return out_feats, grad_feats, grad_w_in, grad_bias, grad_w_out, grad_gain


def solution(mesh):
    placed = (
        P(AXES, None),
        P(AXES, None, None, None),
        P(AXES, None),
        P(),
        P(),
        P(),
        P(),
        P(AXES, None),
    )
    return jax.shard_map(
        per_device,
        mesh=mesh,
        in_specs=placed,
        out_specs=(P(AXES, None), P(AXES, None), P(), P(), P(), P()),
        check_vma=False,
    )
```

```python
import functools
import math

import jax
import jax.numpy as jnp
from jax import lax
from jax.experimental import pallas as pl
from jax.experimental.pallas import tpu as pltpu
from jax.sharding import PartitionSpec as P


HALO = 16
EPS = 1e-05
AXES = ("band", "rep")
F32 = jnp.float32
BF16 = jnp.bfloat16
OUTER = 8
CH = 4
HBM = pl.BlockSpec(memory_space=pltpu.HBM)
ANY = pl.BlockSpec(memory_space=pl.ANY)
SMEM = pl.BlockSpec(memory_space=pltpu.SMEM)
VMEM = pl.BlockSpec(memory_space=pltpu.VMEM)


def nt(a, b):
    return lax.dot_general(a, b, (((1,), (1,)), ((), ())), preferred_element_type=F32)


def nn(a, b):
    return jnp.dot(a, b, preferred_element_type=F32)


def eye(n):
    rows = lax.broadcasted_iota(jnp.int32, (n, n), 0)
    cols = lax.broadcasted_iota(jnp.int32, (n, n), 1)
    return (rows == cols).astype(BF16)


def column(row, width):
    return jnp.transpose(jnp.broadcast_to(row, (width, row.shape[1])))


def lanes(parts):
    return jnp.concatenate(parts, axis=1)


def widen(block, times):
    return lanes([block] * times)


def parity():
    place = lax.axis_index("band") * lax.axis_size("rep") + lax.axis_index("rep")
    return lax.rem(place, 2)


def swap(x, far):
    n = lax.axis_size("band") * lax.axis_size("rep")
    pairs = []
    for c in range(n // 2):
        a, b = (2 * c, 2 * c + 1) if not far else (2 * c + 1, (2 * c + 2) % n)
        pairs += [(a, b), (b, a)]
    return lax.ppermute(x, AXES, pairs)


def rim_at(nb, far):
    odd = parity()
    return (odd if far else 1 - odd) * (HALO + nb)


def quarter(nb, nearest):
    odd = parity()
    q = HALO // 2
    if nearest:
        return odd * (HALO + q), odd * q, q + odd * (nb + q)
    return q + odd * (HALO - q), q - odd * q, odd * (nb + HALO + q)


def rows_at(far):
    odd = parity()
    return (odd if far else 1 - odd) * HALO


def pipelined(count, *stages):
    held = {}
    for t in range(count + len(stages) - 1):
        for i, stage in enumerate(stages):
            if 0 <= t - i < count:
                held[t - i] = stage(t - i, *held.get(t - i, ()))


def for_blocks(count, body, per=4):
    def step(it, c):
        for s in range(per):
            body(it * per + s)
        return c

    lax.fori_loop(0, count // per, step, 0)


def turn_rows(x, ext, out, base, one):
    blk = ext.shape[2]

    def turn(b):
        block = nt(one, x[pl.ds(b * blk, blk)]).astype(BF16)
        ext[HALO + base + b] = block
        out[b] = block

    for_blocks(HALO, turn, 8)


def half_of(x_hbm, x, base, sem):
    rows = x.shape[0]
    return pltpu.make_async_copy(
        x_hbm.at[pl.ds(pl.multiple_of(base * (rows // HALO), rows), rows)], x, sem
    )


def turn_kernel(nb, x_hbm, ext, near_border, outer, x, sem):
    blk = ext.shape[2]
    q = HALO // 2
    starts = [quarter(nb, True)[0], quarter(nb, False)[0]]
    pieces = sem.shape[0]
    per = HALO // pieces

    def get(i):
        rows = per * blk
        first = starts[i * per // q] + i * per % q
        return pltpu.make_async_copy(
            x_hbm.at[pl.ds(pl.multiple_of(first * blk, rows), rows)],
            x.at[pl.ds(i * rows, rows)],
            sem.at[i],
        )

    for i in range(pieces):
        get(i).start()
    one = eye(blk)
    for i in range(pieces):
        get(i).wait()
        for b in range(i * per, (i + 1) * per):
            block = nt(one, x[b * blk : (b + 1) * blk]).astype(BF16)
            ext[HALO + starts[b // q] + b % q] = block
            if b < q:
                near_border[b] = block
            else:
                outer[b - q] = block


def fetch_rims(near_hbm, far_hbm, rims, sem):
    copies = [
        pltpu.make_async_copy(far_hbm, rims.at[pl.ds(rows_at(True), HALO)], sem.at[0]),
        pltpu.make_async_copy(near_hbm, rims.at[pl.ds(rows_at(False), HALO)], sem.at[1]),
    ]
    for c in copies:
        c.start()
    return copies


def take_rim(rim, buf, at):
    def one(b):
        buf[at + b] = rim[b]

    for_blocks(rim.shape[0], one, 8)


def inner_tile(b, ext, tiles, offs, part):
    slot = jnp.where(b < HALO, 2, 1)
    left = lanes([ext[HALO + b], ext[HALO + b + offs[slot, b]]])
    part[b] = nt(left, lanes([tiles[b, 0], tiles[b, slot]]))


def inner0_kernel(
    nb, offs, ext_in, x_hbm, tiles_hbm, w_in_hbm, w_out_hbm, bias_hbm, gain_hbm,
    ext, near, part, w1t, w2t, w2, bcols, gcols, kept, x, tiles, w_in, w_out, bias, gain, sem, tsem,
):
    base = rows_at(False)
    per = nb // tsem.shape[0]

    def get_t(it):
        some = pl.ds(it * per, per)
        return pltpu.make_async_copy(tiles_hbm.at[some], tiles.at[some], tsem.at[it])

    get = half_of(x_hbm, x, base, sem.at[1])
    gets = [
        pltpu.make_async_copy(w_in_hbm, w_in, sem.at[2]),
        pltpu.make_async_copy(w_out_hbm, w_out, sem.at[3]),
        pltpu.make_async_copy(bias_hbm, bias, sem.at[4]),
        pltpu.make_async_copy(gain_hbm, gain, sem.at[5]),
    ]
    get.start()
    for it in range(nb // per):
        get_t(it).start()
    for c in gets:
        c.start()
    one = eye(tiles.shape[2])
    get.wait()
    turn_rows(x, ext, near, base, one)
    keep = pltpu.make_async_copy(ext.at[pl.ds(HALO, nb)], kept, sem.at[0])
    keep.start()

    def step(it, c):
        get_t(it).wait()
        for s in range(per):
            inner_tile(it * per + s, ext, tiles, offs, part)
        return c

    lax.fori_loop(0, nb // per, step, 0)
    for c in gets:
        c.wait()
    for layer in range(w_in.shape[0]):
        w1t[layer] = (0.5 * nt(one, w_in[layer])).astype(BF16)
        w2t[layer] = nt(one, w_out[layer]).astype(BF16)
        w2[layer] = (0.5 * w_out[layer].astype(F32)).astype(BF16)
        bcols[layer] = column(0.5 * bias[layer : layer + 1], bcols.shape[2])
        gcols[layer] = column(gain[layer : layer + 1], gcols.shape[2])
    keep.wait()


def inner1_kernel(nb, offs, ext, tiles, cot, part, cott, acc1, acc0):
    for_blocks(nb, lambda b: inner_tile(b, ext, tiles, offs, part))
    blk = tiles.shape[2]
    one = eye(blk)

    def turn(b):
        cott[b] = nt(one, cot[pl.ds(b * blk, blk)]).astype(BF16)

    for_blocks(nb, turn)
    clear(acc1)
    clear(acc0)


def edge_slot(b):
    return jnp.where(b < HALO, 1, 2)


def join_step(blocks, ext, part, tiles, offs, w1t, bias):
    agg = []
    for b in blocks:
        slot = edge_slot(b)
        agg.append((part[b] + nt(ext[HALO + b + offs[slot, b]], tiles[b, slot])).astype(BF16))
    agg = lanes(agg)
    feats = lanes([ext[HALO + b] for b in blocks])
    half = nn(w1t, jnp.concatenate([feats, agg], axis=0)) + widen(bias[...], CH)
    return feats, agg, half


def mix_step(half, w2t):
    t = jnp.tanh(half)
    up = 1.0 + t
    act = (half * up).astype(BF16)
    slope = up * (1.0 + half * (1.0 - t))
    return act, slope, nn(w2t, act)


def norm_step(feats, mix, gain):
    centred = mix - jnp.mean(mix, axis=0, keepdims=True)
    inv = lax.rsqrt(jnp.mean(centred * centred, axis=0, keepdims=True) + EPS)
    xhat = centred * inv
    after = (feats.astype(F32) + xhat * widen(gain[...], CH)).astype(BF16)
    return xhat, inv, after


def unmix_step(grad, xhat, inv, w2, gain):
    wide = widen(gain[...], CH)
    prod = grad * xhat
    gx = grad * wide
    gmix = inv * (
        gx - jnp.mean(gx, axis=0, keepdims=True) - xhat * jnp.mean(prod * wide, axis=0, keepdims=True)
    )
    gmix = gmix.astype(BF16)
    return prod, gmix, nn(w2, gmix)


def unjoin_step(gact, slope, w1):
    gpre = gact * slope
    gpre_b = gpre.astype(BF16)
    gcat = nn(w1, gpre_b)
    width = gact.shape[0]
    return gpre, gpre_b, gcat[:width], gcat[width:].astype(BF16)


def chunk(base, it):
    return [base + it * CH + s for s in range(CH)]


def cut(wide, s, blk):
    return wide[:, s * blk : (s + 1) * blk]


def fold(wide, blk):
    total = cut(wide, 0, blk)
    for s in range(1, CH):
        total = total + cut(wide, s, blk)
    return total


def push_edge(blocks, gagg, acc, tiles, offs, blk):
    for s, b in enumerate(blocks):
        slot = edge_slot(b)
        acc[HALO + b + offs[slot, b]] += nn(cut(gagg, s, blk), tiles[b, slot])


def push_inner(b, gagg, acc, first, tiles, offs, blk):
    slot = jnp.where(b < HALO, 2, 1)
    both = nn(gagg, lanes([tiles[b, 0], tiles[b, slot]]))
    acc[first + b] += both[:, :blk]
    acc[first + b + offs[slot, b]] += both[:, blk:]


def clear(ref):
    def one(b):
        ref[b] = jnp.zeros(ref.shape[1:], ref.dtype)

    for_blocks(ref.shape[0], one)


def node0_kernel(
    nb, kind, offs, rim, ext_in, part, tiles, w1t, w2t, bcols, gcols, *refs
):
    rim_out, ext, after_ext, agg, act, slope, xhat, inv = refs[{"outer": 0, "nearest": 6, "near": 1}[kind] :]
    bcol, gcol = bcols.at[0], gcols.at[0]
    blk = tiles.shape[2]
    if kind == "near":
        base, local, at = rows_at(False), 0, rim_at(nb, False)
    else:
        base, local, _ = quarter(nb, kind == "nearest")
        at = quarter(nb, kind == "outer")[2]
    take_rim(rim, ext, at)

    def join(it):
        return join_step(chunk(base, it), ext, part, tiles, offs, w1t[0], bcol)

    def mixing(it, feats, agg_w, half):
        for s, b in enumerate(chunk(local, it)):
            agg[b] = cut(agg_w, s, blk)
        return feats, *mix_step(half, w2t[0])

    def norm(it, feats, act_w, slope_w, mix):
        xhat_w, inv_w, after = norm_step(feats, mix, gcol)
        slope_w, xhat_w = slope_w.astype(BF16), xhat_w.astype(BF16)
        for s, b in enumerate(chunk(local, it)):
            act[b] = cut(act_w, s, blk)
            slope[b] = cut(slope_w, s, blk)
            xhat[b] = cut(xhat_w, s, blk)
            inv[b] = cut(inv_w, s, blk)
            after_ext[HALO + base + it * CH + s] = cut(after, s, blk)
            rim_out[it * CH + s] = cut(after, s, blk)

    pipelined(rim_out.shape[0] // CH, join, mixing, norm)


def node1_kernel(
    nb, is_far, offs, rim, ext_in, part, tiles, cott, w1t, w2t, w_in, w2, bcols, gcols, *refs
):
    rim_out, ext, h2, agg, act, gmix, gpre, gagg, acc, gb, gg = refs[2:] if is_far else refs[3:]
    bcol, gcol = bcols.at[1], gcols.at[1]
    blk = tiles.shape[2]
    if is_far:
        gb[...] = jnp.zeros_like(gb)
        gg[...] = jnp.zeros_like(gg)
    if is_far:
        take_rim(rim, ext, quarter(nb, True)[2])
        take_rim(refs[1], ext, quarter(nb, False)[2])
    else:
        take_rim(rim, ext, rim_at(nb, False))
    base = rows_at(is_far)

    def join(it):
        return join_step(chunk(base, it), ext, part, tiles, offs, w1t[1], bcol)

    def mixing(it, feats, agg_w, half):
        for s, b in enumerate(chunk(0, it)):
            agg[b] = cut(agg_w, s, blk)
        return feats, *mix_step(half, w2t[1])

    def turn(it, feats, act_w, slope, mix):
        xhat, inv, after = norm_step(feats, mix, gcol)
        grad = lanes([cott[b] for b in chunk(base, it)]).astype(F32)
        prod, gmix_w, gact = unmix_step(grad, xhat, inv, w2[1], gcol)
        gg[...] += fold(prod, blk)
        for s, b in enumerate(chunk(0, it)):
            act[b] = cut(act_w, s, blk)
            h2[b] = cut(after, s, blk)
            gmix[b] = cut(gmix_w, s, blk)
        return slope, gact

    def unjoin(it, slope, gact):
        gpre_f, gpre_w, gh, gagg_w = unjoin_step(gact, slope, w_in[1])
        gb[...] += fold(gpre_f, blk)
        grad = lanes([cott[b] for b in chunk(base, it)]).astype(F32)
        return gpre_w, grad + gh, gagg_w

    def push(it, gpre_w, rest, gagg_w):
        for s, b in enumerate(chunk(0, it)):
            gpre[b] = cut(gpre_w, s, blk)
            gagg[b] = cut(gagg_w, s, blk)
            acc[HALO + base + b] += cut(rest, s, blk)
        push_edge(chunk(base, it), gagg_w, acc, tiles, offs, blk)

    pipelined(HALO // CH, join, mixing, turn, unjoin, push)
    at = rim_at(nb, is_far)

    def give(b):
        rim_out[b] = acc[at + b].astype(BF16)

    for_blocks(HALO, give, 8)


def outer_step(local, feats, first, agg, act, gmix, gpre, gw):
    width = feats.shape[1]
    gpre_w = lanes([gpre[b] for b in local])
    gw[0:width] += nt(lanes([feats[first + b] for b in local]), gpre_w)
    gw[width : 2 * width] += nt(lanes([agg[b] for b in local]), gpre_w)
    gw[2 * width :] += nt(lanes([act[b] for b in local]), lanes([gmix[b] for b in local]))


def row_sum(block):
    return jnp.sum(jnp.transpose(block), axis=0, keepdims=True)


def weights_kernel(offs, acc_in, tiles, ext, gb, gg, *refs):
    halves, (acc, gw, gv, h2_hbm, sem) = (refs[:6], refs[6:12]), refs[12:]
    blk = tiles.shape[2]
    puts = [
        pltpu.make_async_copy(half[0], h2_hbm.at[pl.ds(rows_at(is_far), HALO)], sem.at[i])
        for i, (is_far, half) in enumerate(zip((True, False), halves))
    ]
    for c in puts:
        c.start()
    gv[0:1] = row_sum(gb[...])
    gv[1:2] = row_sum(gg[...])
    gw[...] = jnp.zeros_like(gw)
    for is_far, (_, agg, act, gmix, gpre, gagg) in zip((True, False), halves):
        base = rows_at(is_far)
        for_blocks(HALO, lambda b: push_inner(base + b, gagg[b], acc, HALO, tiles, offs, blk))

        def outer(it, c):
            local = [it * OUTER + s for s in range(OUTER)]
            outer_step(local, ext, HALO + base, agg, act, gmix, gpre, gw)
            return c

        lax.fori_loop(0, HALO // OUTER, outer, 0)
    for c in puts:
        c.wait()


def output_kernel(nb, h_hbm, out_hbm, h, out, sem):
    blk = h.shape[2]
    per = nb // sem.shape[0]

    def get(it):
        some = pl.ds(it * per, per)
        return pltpu.make_async_copy(h_hbm.at[some], h.at[some], sem.at[it])

    def put(it):
        rows = pl.ds(pl.multiple_of(it * per * blk, per * blk), per * blk)
        return pltpu.make_async_copy(out.at[rows], out_hbm.at[rows], sem.at[it])

    for it in range(nb // per):
        get(it).start()
    one = eye(blk)

    def step(it, c):
        get(it).wait()
        for s in range(per):
            b = it * per + s
            out[pl.ds(pl.multiple_of(b * blk, blk), blk)] = nt(one, h[b]).astype(BF16)
        put(it).start()
        return c

    lax.fori_loop(0, nb // per, step, 0)
    for it in range(nb // per):
        put(it).wait()


def node2_kernel(nb, is_far, offs, rim, acc_in, tiles, w_in, w2, gcols, kept, agg, act, slope, xhat, inv, *refs):
    if is_far:
        (gw1, gv1, *_, far_hbm, bundle_hbm, gagg_hbm, acc_hbm,
         acc, gb, gg, gw, gagg, gmix, gpre, rims, bundle, sem) = refs
    else:
        _, acc, gb, gg, gw, gagg_hbm, near_hbm, gagg, gmix, gpre, rims, sem = refs
        gb[...] = jnp.zeros_like(gb)
        gg[...] = jnp.zeros_like(gg)
        gw[...] = jnp.zeros_like(gw)
    blk = tiles.shape[2]
    gcol = gcols.at[0]
    base = rows_at(is_far)

    def unmix(it):
        local = chunk(0, it)
        grad = lanes([acc_in[HALO + base + b] + rim[b].astype(F32) for b in local])
        xhat_w = lanes([xhat[b] for b in local]).astype(F32)
        inv_w = lanes([inv[b] for b in local])
        prod, gmix_w, gact = unmix_step(grad, xhat_w, inv_w, w2[0], gcol)
        gg[...] += fold(prod, blk)
        for s, b in enumerate(local):
            gmix[b] = cut(gmix_w, s, blk)
        return gact, grad

    def unjoin(it, gact, grad):
        slope_w = lanes([slope[b] for b in chunk(0, it)]).astype(F32)
        gpre_f, gpre_w, gh, gagg_w = unjoin_step(gact, slope_w, w_in[0])
        gb[...] += fold(gpre_f, blk)
        return gpre_w, grad + gh, gagg_w

    def push(it, gpre_w, rest, gagg_w):
        for s, b in enumerate(chunk(0, it)):
            gpre[b] = cut(gpre_w, s, blk)
            gagg[b] = cut(gagg_w, s, blk)
            acc[HALO + base + b] += cut(rest, s, blk)
        some = pl.ds(it * CH, CH)
        pltpu.make_async_copy(gagg.at[some], gagg_hbm.at[some], sem.at[1]).start()
        push_edge(chunk(base, it), gagg_w, acc, tiles, offs, blk)
        if (it + 1) * CH % OUTER == 0:
            wide = list(range((it + 1) * CH - OUTER, (it + 1) * CH))
            outer_step(wide, kept, base, agg, act, gmix, gpre, gw)

    pipelined(HALO // CH, unmix, unjoin, push)
    at = rim_at(nb, is_far)

    def rim_sum(b):
        rims[b] = acc[at + b].astype(BF16)

    if is_far:
        put = pltpu.make_async_copy(acc.at[pl.ds(HALO, nb)], acc_hbm, sem.at[0])
        put.start()
    for_blocks(HALO, rim_sum, 8)
    sent = pltpu.make_async_copy(rims, far_hbm if is_far else near_hbm, sem.at[2])
    sent.start()
    if not is_far:
        pltpu.make_async_copy(gagg, gagg_hbm, sem.at[1]).wait()
        sent.wait()
        return
    devices = bundle.shape[0]
    rows = gw.shape[0]
    share = 2 * rows // devices
    vectors = jnp.concatenate([row_sum(gb[...]), row_sum(gg[...]), gv1[...]], axis=0)
    vectors = jnp.concatenate([vectors, jnp.zeros_like(vectors)], axis=0).astype(BF16)
    for p in range(devices):
        bundle[p, 0:8] = vectors
        first = p * share
        if first + share <= rows:
            mine = gw[first : first + share]
        elif first >= rows:
            mine = gw1[first - rows : first - rows + share]
        else:
            mine = jnp.concatenate([gw[first:rows], gw1[0 : first + share - rows]], axis=0)
        bundle[p, 8 : 8 + share] = mine.astype(BF16)
    out = pltpu.make_async_copy(bundle, bundle_hbm, sem.at[3])
    out.start()
    pltpu.make_async_copy(gagg, gagg_hbm, sem.at[1]).wait()
    for c in [sent, put, out]:
        c.wait()


def total_kernel(scale, parts, mine_hbm, gbias, ggain, mine, sem):
    total = jnp.sum(parts[...].astype(F32), axis=0) * scale
    mine[...] = jnp.broadcast_to(total[8:][None], mine.shape).astype(BF16)
    put = pltpu.make_async_copy(mine, mine_hbm, sem.at[0])
    put.start()
    gbias[0:1] = total[0:1]
    ggain[0:1] = total[1:2]
    gbias[1:2] = total[2:3]
    ggain[1:2] = total[3:4]
    put.wait()


def final_kernel(
    nb, offs, near, far, acc_hbm, gagg_far, gagg_near, tiles_hbm, out_hbm,
    acc, gagg, tiles, halo, out, sem, tsem,
):
    blk = tiles.shape[2]
    per = nb // tsem.shape[0]
    get_a = pltpu.make_async_copy(acc_hbm, acc, sem.at[0])

    def get_t(it):
        some = pl.ds(it * per, per)
        return pltpu.make_async_copy(tiles_hbm.at[some], tiles.at[some], tsem.at[it])

    get_g = fetch_rims(gagg_near, gagg_far, gagg, sem.at[pl.ds(4, 2)])
    get_a.start()
    for it in range(nb // per):
        get_t(it).start()
    rims = fetch_rims(near, far, halo, sem.at[pl.ds(2, 2)])
    for c in get_g:
        c.wait()
    get_a.wait()

    def push(it, c):
        get_t(it).wait()
        for s in range(per):
            push_inner(it * per + s, gagg[it * per + s], acc, 0, tiles, offs, blk)
        return c

    lax.fori_loop(0, nb // per, push, 0)

    for c in rims:
        c.wait()

    def put(it):
        rows = pl.ds(it * per * blk, per * blk)
        return pltpu.make_async_copy(out.at[rows], out_hbm.at[rows], tsem.at[it])

    def step(it, c):
        for s in range(per):
            b = it * per + s
            out[pl.ds(b * blk, blk)] = jnp.transpose(acc[b] + halo[b].astype(F32))
        put(it).start()
        return c

    lax.fori_loop(0, nb // per, step, 0)
    for it in range(nb // per):
        put(it).wait()


def unpack_kernel(sums, out1_hbm, out2_hbm, out1, out2, sem):
    devices, share, _ = sums.shape
    _, upper, _ = out1.shape
    rows = upper + out2.shape[1]
    for p in range(devices):
        mine = sums[p].astype(F32)
        at = p * share
        while at < (p + 1) * share:
            layer, row = divmod(at, rows)
            end = min((p + 1) * share, layer * rows + (upper if row < upper else rows))
            piece = mine[at - p * share : end - p * share]
            if row < upper:
                out1[layer, row : row + end - at] = piece
            else:
                out2[layer, row - upper : row - upper + end - at] = piece
            at = end
    puts = [
        pltpu.make_async_copy(out1, out1_hbm, sem.at[0]),
        pltpu.make_async_copy(out2, out2_hbm, sem.at[1]),
    ]
    for p in puts:
        p.start()
    for p in puts:
        p.wait()


def call(body, args, outs, scratch=(), alias=None, far_args=(), any_args=(), flops=0, moved=0):
    args = [
        pltpu.with_memory_space_constraint(a, pltpu.HBM) if i in far_args else a
        for i, a in enumerate(args)
    ]
    return pl.pallas_call(
        body,
        in_specs=[
            HBM if i in far_args else ANY if i in any_args else SMEM if a.dtype == jnp.int32 else VMEM
            for i, a in enumerate(args)
        ],
        out_specs=[HBM if len(o) == 3 else VMEM for o in outs],
        out_shape=[
            pltpu.HBM(o[0], o[1]) if len(o) == 3 else jax.ShapeDtypeStruct(o[0], o[1]) for o in outs
        ],
        scratch_shapes=list(scratch),
        input_output_aliases=alias or {},
        compiler_params=pltpu.CompilerParams(vmem_limit_bytes=24 << 20),
        cost_estimate=pl.CostEstimate(flops=flops, bytes_accessed=moved, transcendentals=0),
    )(*args)


def dma(n):
    return pltpu.SemaphoreType.DMA((n,))


def per_device(feats, tile_vals, tile_offs, w_in, bias_in, w_out, gain, cot):
    nodes, width = feats.shape
    nb, slots, blk, _ = tile_vals.shape
    hid = w_out.shape[1]
    layers = w_in.shape[0]
    assert nb == 2 * HALO and width == blk and hid == width and layers == 2
    devices = lax.axis_size("band") * lax.axis_size("rep")
    block = (width, blk)
    full, _, ext = ((n, *block) for n in (nb, HALO, nb + 2 * HALO))
    whole = (2 * width + hid, hid)
    share = layers * whole[0] // devices
    assert share * devices == layers * whole[0]
    v = pltpu.VMEM
    part_of = functools.partial
    tile_flops = 2 * blk * blk * width
    mlp_flops = 2 * nodes * (2 * width * hid + hid * width)
    mib = 2 * nodes * width
    offs = tile_offs.T

    half = (HALO, *block)
    half_rows = (nodes // 2, width)

    some = (HALO // 2, *block)
    h0, border, outer = call(
        part_of(turn_kernel, nb), (feats,), [(ext, BF16), (some, BF16), (some, BF16)],
        [v(half_rows, BF16), dma(4)], far_args=(0,),
        flops=nb * tile_flops, moved=3 * mib,
    )
    border = swap(border, True)
    outer = swap(outer, True)
    h0, near, part, w1t, w2t, w2, bcols, gcols, kept = call(
        part_of(inner0_kernel, nb), (offs, h0, feats, tile_vals, w_in, w_out, bias_in, gain),
        [(ext, BF16), (half, BF16), (full, F32), ((layers, hid, 2 * width), BF16), ((layers, width, hid), BF16),
         (w_out.shape, BF16), ((layers, *block), F32), ((layers, *block), F32), (full, BF16, True)],
        [v(half_rows, BF16), v(tile_vals.shape, BF16), v(w_in.shape, BF16), v(w_out.shape, BF16), v(bias_in.shape, F32), v(gain.shape, F32), dma(6), dma(8)],
        {1: 0}, far_args=(2, 3, 4, 5, 6, 7),
        flops=2 * nb * tile_flops, moved=6 * mib,
    )
    near = swap(near, False)

    def node0(kind, rim, h, more):
        alias = {2: 1} | {9 + i: 2 + i for i in range(len(more))}
        return call(
            part_of(node0_kernel, nb, kind),
            (offs, rim, h, part, tile_vals, w1t, w2t, bcols, gcols, *more),
            [(rim.shape, BF16), (ext, BF16), (ext, BF16), *[(half, BF16)] * 4, ((HALO, 1, blk), F32)],
            alias=alias,
            flops=(nb * tile_flops + mlp_flops) // 4, moved=4 * mib,
        )

    next_outer, h0, *saved_far = node0("outer", border, h0, ())
    next_outer = swap(next_outer, True)
    border, h0, *saved_far = node0("nearest", outer, h0, saved_far)
    border = swap(border, True)
    near, h0, h1, *saved_near = node0("near", near, h0, saved_far[:1])
    saved_far = saved_far[1:]
    near = swap(near, False)
    part, cott, acc1, acc0 = call(
        part_of(inner1_kernel, nb), (offs, h1, tile_vals, cot), [(full, F32), (full, BF16), (ext, F32), (ext, F32)],
        flops=2 * nb * tile_flops, moved=8 * mib,
    )

    def node1(is_far, rim, h, more):
        return call(
            part_of(node1_kernel, nb, is_far),
            (offs, rim, h, part, tile_vals, cott, w1t, w2t, w_in, w2, bcols, gcols, *more),
            [(half, BF16), (ext, BF16), *[(half, BF16)] * 6, (ext, F32), (block, F32), (block, F32)],
            alias={2: 1, 12: 8} if is_far else {2: 1, 12: 8, 13: 9, 14: 10},
            flops=nb * tile_flops + mlp_flops, moved=8 * mib,
        )

    far, h1, *made_far, acc, gb1, gg1 = node1(True, border, h1, (acc1, next_outer))
    far = swap(far, True)
    near, h1, *made_near, acc, gb1, gg1 = node1(False, near, h1, (acc, gb1, gg1))
    near = swap(near, False)
    acc, gw1, gv1, h2 = call(
        weights_kernel, (offs, acc, tile_vals, h1, gb1, gg1, *made_far, *made_near),
        [(ext, F32), (whole, F32), ((2, hid), F32), (full, BF16, True)],
        [dma(2)], {1: 0},
        flops=tile_flops, moved=mib,
    )

    def node2(is_far, rim, acc, saved, more, outs, scratch, alias):
        return call(
            part_of(node2_kernel, nb, is_far),
            (offs, rim, acc, tile_vals, w_in, w2, gcols, kept, *saved, *more), outs, scratch, alias,
            flops=nb * tile_flops + mlp_flops, moved=8 * mib,
        )

    sums = [(ext, F32), (block, F32), (block, F32), (whole, F32)]
    work = [v(half, BF16)] * 4
    *state, gagg_near, near = node2(
        False, near, acc, saved_near, (acc0,), [*sums, (half, BF16, True), (half, BF16, True)], [*work, dma(3)], {13: 0}
    )
    far, bundle, gagg_far, acc, *_ = node2(
        True, far, acc, saved_far, (gw1, gv1, *state),
        [(half, BF16, True), ((devices, 8 + share, hid), BF16, True), (half, BF16, True), (full, F32, True), *sums],
        [*work, v((devices, 8 + share, hid), BF16), dma(4)],
        {15 + i: 4 + i for i in range(4)},
    )

    parts = lax.all_to_all(bundle, AXES, 0, 0, tiled=True)
    near, far = swap(near, False), swap(far, True)
    (out_feats,) = call(
        part_of(output_kernel, nb), (h2,), [((nodes, width), BF16, True)],
        [v(full, BF16), v((nodes, width), BF16), dma(4)], far_args=(0,),
        flops=nb * tile_flops, moved=2 * mib,
    )
    mine, grad_bias, grad_gain = call(
        part_of(total_kernel, 1.0 / math.sqrt(nodes * devices)), (parts,),
        [((devices, share, hid), BF16, True), ((layers, hid), F32), ((layers, width), F32)],
        [v((devices, share, hid), BF16), dma(1)],
        flops=nodes * width, moved=mib,
    )
    sums = lax.all_to_all(mine, AXES, 0, 0, tiled=True)
    (grad_feats,) = call(
        part_of(final_kernel, nb), (offs, near, far, acc, gagg_far, gagg_near, tile_vals),
        [((nodes, width), F32, True)],
        [v(full, F32), v(full, BF16), v((nb, slots, blk, blk), BF16), v(full, BF16), v((nodes, width), F32), dma(6), dma(8)],
        far_args=(3, 4, 5, 6), any_args=(1, 2),
        flops=2 * nb * tile_flops, moved=9 * mib,
    )
    grad_w_in, grad_w_out = call(
        unpack_kernel, (sums,),
        [((layers, 2 * width, hid), F32, True), ((layers, hid, width), F32, True)],
        [v((layers, 2 * width, hid), F32), v((layers, hid, width), F32), dma(2)],
        flops=nodes * width, moved=mib,
    )
    return out_feats, grad_feats, grad_w_in, grad_bias, grad_w_out, grad_gain


def solution(mesh):
    placed = (
        P(AXES, None),
        P(AXES, None, None, None),
        P(AXES, None),
        P(),
        P(),
        P(),
        P(),
        P(AXES, None),
    )
    return jax.shard_map(
        per_device,
        mesh=mesh,
        in_specs=placed,
        out_specs=(P(AXES, None), P(AXES, None), P(), P(), P(), P()),
        check_vma=False,
    )
```
